256 devices in a mesh: seq: 64 (over y, z_hi, x, core), ch: 4 (over z_lo).
Axes of the slice: x: 4, y: 4, z: 8 (z_hi: 2, z_lo: 4; z = z_hi * 4 + z_lo), core: 2. Of those that a mesh axis runs over, the one named last changes fastest.
Arguments:
- token_ids: int32 [8192], P('seq'), may hold values from 0 to 511
- embedding: bfloat16 [512, 4096], P(None, 'ch'), may hold values from -6 to 6
- short_filter: float32 [7, 4096], P(None, 'ch'), may hold values from -2 to 2
- medium_filter: float32 [128, 4096], P(None, 'ch'), may hold values from -0.5 to 0.5
- long_residue: float32 [16, 4096], P(None, 'ch'), may hold values from -10.5 to 10.5, as said below
- long_rate: float32 [16, 4096], P(None, 'ch'), may hold values from 1e-05 to 0.05
- query_gain: float32 [4096], P('ch'), may hold values from -14 to 14
- key_gain: float32 [4096], P('ch'), may hold values from -14 to 14
Outputs:
- hyena_out: bfloat16 [8192, 4096], P('seq', 'ch')
- attended: bfloat16 [8192, 4096], P('seq', 'ch')
The draws below stay inside these ranges and needn't reach their ends.
Inputs may be any that keep to these rules, and one draw needn't show every extreme that they name: `long_residue`: residues of the long filter's modes.
All inputs are finite; a program needn't handle non-finite values.
Results may differ from the reference program's by a relative error of at most 0.0095.
The reference program's roundings to bfloat16 on the way count: a program that leaves them out, or rounds other values in their place, can miss the bound.
Values may be sent and summed in bfloat16 or wider, within the bound.
A program may use at most 64 MiB of HBM per device.

```python
import math
import jax
import jax.numpy as jnp
import numpy as np
from jax import lax

C = 4096
HEAD = 128
VOCAB = 512
SHORT = 7
MEDIUM = 128
ORDER = 16
HEADS = 32
LENGTH = 8192


def draw_long_rate(key, part):
    fraction = jax.random.uniform(key, (ORDER, C), jnp.float32)
    log_low = math.log(1e-05)
    log_high = math.log(0.05)
    return jnp.exp(log_low + fraction * (log_high - log_low))


def draw_long_residue(key, part):
    channel_ramp = 1.0 + 0.75 * jnp.arange(C, dtype=jnp.float32) / C
    entries = jnp.clip(jax.random.normal(key, (ORDER, C), jnp.float32), -6.0, 6.0)
    return entries * channel_ramp[None, :]


def gain_pair(key):
    folded = jax.random.fold_in(key, 11)
    key_one, key_two = jax.random.split(folded, 2)
    query_draw = jnp.clip(1.4 * jax.random.normal(key_one, (C,), jnp.float32), -14.0, 14.0)
    key_draw = jnp.clip(1.4 * jax.random.normal(key_two, (C,), jnp.float32), -14.0, 14.0)
    return (query_draw, key_draw)


def draw_query_gain(key, part):
    return gain_pair(key)[0]


def draw_key_gain(key, part):
    return gain_pair(key)[1]


def with_ends(values, stream_key, least, high):
    place = [jax.random.randint(jax.random.fold_in(stream_key, axis), (), 0, length) for axis, length in enumerate(values.shape)]
    widest = values.shape.index(max(values.shape))
    neighbour = place[:widest] + [(place[widest] + 1) % values.shape[widest]] + place[widest + 1:]
    return values.at[tuple(place)].set(least).at[tuple(neighbour)].set(high)


def levels(stream_key, dims, cuts, low, top_value):
    gain = 1.0
    for position, shards_of in cuts:
        steps = jax.random.uniform(jax.random.fold_in(jax.random.fold_in(stream_key, 6), position), (shards_of,), jnp.float32, low / len(cuts), top_value / len(cuts))
        gain = gain * jnp.repeat(jnp.exp(steps), dims[position] // shards_of).reshape((-1,) + (1,) * (len(dims) - 1 - position))
    return gain


def cumulative_ranks(amount, skew):
    loads = [(1 << 20) // math.isqrt(standing ** skew) + 1 for standing in range(1, amount + 1)]
    spread = 1 + sum(loads) // (1 << 30)
    return np.cumsum(np.array([max(1, weight // spread) for weight in loads]))


def skewed_ids(rng, shape, amount, slope):
    grid = cumulative_ranks(amount, slope)
    pick = jax.random.randint(jax.random.fold_in(rng, 1), shape, 0, int(grid[amount - 1]))
    grade = jnp.searchsorted(jnp.asarray(grid, jnp.int32), pick, side="right")
    return jax.random.permutation(jax.random.fold_in(rng, 2), amount)[grade].astype(jnp.int32)


def gaussian(key, dims, width, reach, pieces=(), kind=jnp.bfloat16):
    drawn = jax.random.normal(key, dims, jnp.float32) * width
    if len(pieces) > 0:
        drawn = levels(key, dims, pieces, -0.22, 0.18) * drawn
    return jnp.clip(drawn, min=-reach, max=reach).astype(kind)


def setup_inputs(seed: int = 0) -> dict:
    seeds = jax.random.split(jax.random.key(seed), 9)
    return {
        "token_ids": with_ends(skewed_ids(seeds[0], (LENGTH,), VOCAB, 2), jax.random.fold_in(seeds[0], 3), 0, VOCAB - 1).astype(jnp.int32),
        "embedding": gaussian(seeds[1], (VOCAB, C), 1.0, 6.0, ((1, 4),)),
        "short_filter": gaussian(seeds[2], (SHORT, C), SHORT ** -0.5, 2.0, ((1, 4),), jnp.float32),
        "medium_filter": gaussian(seeds[3], (MEDIUM, C), MEDIUM ** -0.5, 0.5, ((1, 4),), jnp.float32),
        "long_residue": draw_long_residue(jax.random.fold_in(seeds[8], 71), 0),
        "long_rate": draw_long_rate(jax.random.fold_in(seeds[8], 71), 0),
        "query_gain": draw_query_gain(jax.random.fold_in(seeds[8], 71), 0),
        "key_gain": draw_key_gain(jax.random.fold_in(seeds[8], 71), 0),
    }


def rounded(value):
    return lax.optimization_barrier(value.astype(jnp.bfloat16))

def depthwise_conv(signal, tap_weights):
    tap_count = tap_weights.shape[0]
    row_count = signal.shape[0]
    padded = jnp.pad(signal, ((tap_count - 1, 0), (0, 0)))

    def add_tap(tap_index, running):
        start_row = (tap_count - 1 - tap_index).astype(jnp.int32)
        window = lax.dynamic_slice_in_dim(padded, start_row, row_count, 0)
        return running + tap_weights[tap_index] * window
    return lax.fori_loop(0, tap_count, add_tap, jnp.zeros(signal.shape, jnp.float32))

def long_kernel(long_residue, long_rate, length):
    positions = jnp.arange(length, dtype=jnp.int32).astype(jnp.float32)

    def add_mode(mode_index, running):
        decay_rate = long_rate[mode_index]
        mode_weight = long_residue[mode_index] * jnp.sqrt(-jnp.expm1(-2.0 * decay_rate)) / math.sqrt(ORDER)
        return running + mode_weight[None, :] * jnp.exp(-decay_rate[None, :] * positions[:, None])
    return lax.fori_loop(0, ORDER, add_mode, jnp.zeros((length, long_rate.shape[1]), jnp.float32))

def attend_head(operands):
    query_rows, key_rows, value_rows = operands
    length = query_rows.shape[0]
    block_rows = math.gcd(length, 1024)
    score_scale = HEAD ** (-0.5)
    key_index = jnp.arange(length, dtype=jnp.int32)

    def one_block(block_index):
        start_row = block_index * block_rows
        query_part = lax.dynamic_slice_in_dim(query_rows, start_row, block_rows, 0)
        scores = jnp.dot(query_part, key_rows.T, preferred_element_type=jnp.float32) * score_scale
        query_index = start_row + jnp.arange(block_rows, dtype=jnp.int32)
        scores = jnp.where(key_index[None, :] <= query_index[:, None], scores, -1e+30)
        row_peak = lax.optimization_barrier(jnp.max(scores, axis=1, keepdims=True))
        weights = jnp.exp(scores - row_peak)
        row_total = lax.optimization_barrier(jnp.sum(weights, axis=1, keepdims=True))
        blended = jnp.dot(weights.astype(jnp.bfloat16), value_rows, preferred_element_type=jnp.float32)
        return blended / row_total
    outputs = lax.map(one_block, jnp.arange(length // block_rows, dtype=jnp.int32))
    return outputs.reshape(length, value_rows.shape[1])

def reference(token_ids, embedding, short_filter, medium_filter, long_residue, long_rate, query_gain, key_gain):
    embedded = embedding[token_ids]
    embed_float = embedded.astype(jnp.float32)
    short_gated = rounded(embed_float * depthwise_conv(embed_float, short_filter))
    gated_float = short_gated.astype(jnp.float32)
    medium_gated = rounded(gated_float * depthwise_conv(gated_float, medium_filter))
    medium_float = medium_gated.astype(jnp.float32)
    kernel = long_kernel(long_residue, long_rate, LENGTH)
    full_size = 2 * LENGTH
    spectrum = jnp.fft.rfft(medium_float, n=full_size, axis=0) * jnp.fft.rfft(kernel, n=full_size, axis=0)
    long_part = jnp.fft.irfft(spectrum, n=full_size, axis=0)[:LENGTH]
    hyena_out = rounded(medium_float * long_part)
    hyena_float = hyena_out.astype(jnp.float32)
    inverse_scale = lax.rsqrt(lax.optimization_barrier(jnp.sum(hyena_float * hyena_float, axis=1)) / C + 1e-05)
    normed = hyena_float * inverse_scale[:, None]
    values = normed.astype(jnp.bfloat16)
    queries = (normed * query_gain[None, :]).astype(jnp.bfloat16)
    key_rows = (normed * key_gain[None, :]).astype(jnp.bfloat16)
    query_heads = queries.reshape(LENGTH, HEADS, HEAD).transpose(1, 0, 2)
    key_heads = key_rows.reshape(LENGTH, HEADS, HEAD).transpose(1, 0, 2)
    value_heads = values.reshape(LENGTH, HEADS, HEAD).transpose(1, 0, 2)
    outputs = lax.map(attend_head, (query_heads, key_heads, value_heads))
    attended = outputs.transpose(1, 0, 2).reshape(LENGTH, C).astype(jnp.bfloat16)
    return (hyena_out, attended)
```

```python
import math

import jax
import jax.numpy as jnp
from jax import lax
from jax.experimental import pallas as pl
from jax.experimental.pallas import tpu as pltpu
from jax.sharding import PartitionSpec as P

C = 4096
HEAD = 128
EPS = 1e-05
TOK = 128
BLOCKS = 8
SLOT = 144
MESH = pl.DeviceIdType.MESH
F32 = jnp.float32
BF16 = jnp.bfloat16
LIMIT = 60 << 20


def rows_of(step):
    return pl.ds(pl.multiple_of(8 * step, 8), 128)


def front_body(tok_ref, emb_ref, short_ref, med_ref, res_ref, rate_ref, mg_s, yl_s, end_s, lam_s, e_s, sg_s, sw_s, mw_s, cf_s):
    for c in range(BLOCKS):
        lanes = slice(c * 128, (c + 1) * 128)
        sw_s[pl.ds(c, 7, stride=8), :] = short_ref[:, lanes]
        mw_s[pl.ds(c, 128, stride=8), :] = med_ref[:, lanes]
        lam_s[pl.ds(c, 16, stride=8), :] = rate_ref[:, lanes]
        cf_s[pl.ds(c, 16, stride=8), :] = res_ref[:, lanes]
    rate = lam_s[...]
    twice = 2.0 * rate
    tail = jnp.ones_like(twice)
    for k in range(9, 1, -1):
        tail = 1.0 - twice * (1.0 / k) * tail
    cf_s[...] = cf_s[...] * jnp.sqrt(twice * tail) * 0.25
    lam_s[...] = jnp.exp(-rate)

    columns = []
    for k in range(3):
        row = tok_ref[k : k + 1, :].astype(F32)
        columns.append(jnp.broadcast_to(row, (128, 128)).T)
    column = jnp.concatenate([columns[0][112:], columns[1], columns[2]], axis=0)
    lane = lax.broadcasted_iota(jnp.int32, column.shape, 1).astype(F32)
    one_hot = jnp.concatenate(
        [jnp.where(column == lane + 128.0 * k, 1.0, 0.0).astype(BF16) for k in range(4)], axis=1
    )
    for pair in range(4):
        part = jnp.dot(one_hot, emb_ref[:, pair * 256 : pair * 256 + 256], preferred_element_type=F32)
        for k in range(2):
            e_s[pl.ds(2 * pair + k, 272, stride=8), :] = part[:, k * 128 : k * 128 + 128]

    def short_block(block, _):
        first = 16 + block * 16
        own = e_s[rows_of(first), :].reshape(16, 8, 128)
        total = own * sw_s[0:8, :]
        for j in range(1, 7):
            total = total + e_s[rows_of(first - j), :].reshape(16, 8, 128) * sw_s[8 * j : 8 * j + 8, :]
        gated = (own * total).astype(BF16).astype(F32)
        sg_s[rows_of(16 * block), :] = gated.reshape(128, 128)
        return 0

    lax.fori_loop(0, 16, short_block, 0)

    def medium_block(block, _):
        def taps(chunk, total):
            base = 128 + 16 * block - 16 * chunk - 15
            window = sg_s[pl.ds(pl.multiple_of(8 * base, 8), 31 * 8), :].reshape(31, 8, 128)
            weight = mw_s[rows_of(16 * chunk), :].reshape(16, 8, 128)
            for j in range(16):
                total = total + weight[j][None] * window[15 - j : 31 - j]
            return total

        total = lax.fori_loop(0, 8, taps, jnp.zeros((16, 8, 128), F32))
        own = sg_s[rows_of(128 + 16 * block), :].reshape(16, 8, 128)
        gated = (own * total).astype(BF16).astype(F32)
        mg_s[rows_of(16 * block), :] = gated.reshape(128, 128)
        return 0

    lax.fori_loop(0, 8, medium_block, 0)

    lam = lam_s[...].reshape(16, 8, 128)
    coef = cf_s[...].reshape(16, 8, 128)

    def step(block, state):
        for k in range(4):
            tile = pl.ds(pl.multiple_of(8 * (4 * block + k), 8), 8)
            state = lam * state + coef * mg_s[tile, :][None]
            yl_s[tile, :] = jnp.sum(state, axis=0)
        return state

    state = lax.fori_loop(0, 32, step, jnp.zeros((16, 8, 128), F32))
    for r in range(16):
        end_s[pl.ds(r, 8, stride=16), :] = state[r]


def front_kernel(*refs):
    front_body(*refs)


def here():
    seq = lax.axis_index("seq")
    return seq, seq // 8, lax.rem(seq, 8)


def remote(source, target, send, receive, **where):
    return pltpu.make_async_remote_copy(
        src_ref=source, dst_ref=target, send_sem=send, recv_sem=receive, device_id=where, device_id_type=MESH
    )


def greet(names):
    barrier = pltpu.get_barrier_semaphore()
    for where in names:
        pl.semaphore_signal(barrier, inc=1, device_id=where, device_id_type=MESH)
    pl.semaphore_wait(barrier, len(names))


def middle_body(
    rate_ref, mg_s, yl_s, end_s, lam_s, hy_ref, xf_ref,
    got1, got2, got3, pre_s, group_s, h_s, xt_s, inv_s, ss_s,
    send1, recv1, send2, recv2, send3, recv3, sendc, recvc, senda, sendi, recvi, sendx, sends, recvx,
):
    seq, g, i = here()
    ch = lax.axis_index("ch")
    mine = [pl.ds(pl.multiple_of(16 * k, 16), 16) for k in range(8)]

    def part(k):
        return pl.ds(pl.multiple_of(16 * k, 16), 16)

    scans = []
    for d in range(1, 8):
        k = lax.rem(i + d, 8)
        copy = remote(end_s.at[part(k), :], got1.at[part(i), :], send1.at[d], recv1.at[d], seq=8 * g + k)
        copy.start()
        scans.append(copy)
    got1[part(i), :] = end_s[part(i), :]
    rate = rate_ref[:, pl.ds(pl.multiple_of(128 * i, 128), 128)]
    block_decay = jnp.exp(-128.0 * rate)
    group_decay = jnp.exp(-1024.0 * rate)
    for copy in scans:
        copy.wait()
    running = jnp.zeros((16, 128), F32)
    for k in range(8):
        pre_s[16 * k : 16 * k + 16, :] = running
        running = block_decay * running + got1[16 * k : 16 * k + 16, :]
    group_s[...] = running
    scans = []
    for d in range(1, 8):
        k = lax.rem(g + d, 8)
        copy = remote(group_s, got2.at[part(g), :], send2.at[d], recv2.at[d], seq=8 * k + i)
        copy.start()
        scans.append(copy)
    got2[part(g), :] = running
    for copy in scans:
        copy.wait()
    before = jnp.zeros((16, 128), F32)
    for k in range(8):
        before = jnp.where(k < g, group_decay * before + got2[16 * k : 16 * k + 16, :], before)
    for k in range(8):
        pre_s[16 * k : 16 * k + 16, :] = pre_s[16 * k : 16 * k + 16, :] + before
        before = before * block_decay
    scans = []
    for d in range(1, 8):
        k = lax.rem(i + d, 8)
        copy = remote(pre_s.at[part(k), :], got3.at[part(i), :], send3.at[d], recv3.at[d], seq=8 * g + k)
        copy.start()
        scans.append(copy)
    got3[part(i), :] = pre_s[part(i), :]
    for copy in scans:
        copy.wait()

    lam = lam_s[...].reshape(16, 8, 128)
    state = jnp.stack([got3[pl.ds(r, 8, stride=16), :] for r in range(16)], axis=0)

    def step(block, state):
        for k in range(4):
            tile = pl.ds(pl.multiple_of(8 * (4 * block + k), 8), 8)
            state = lam * state
            full = yl_s[tile, :] + jnp.sum(state, axis=0)
            h_s[tile, :] = (mg_s[tile, :] * full).astype(BF16).astype(F32)
        return state

    lax.fori_loop(0, 32, step, state)

    squares = jnp.zeros((128, 128), F32)
    for c in range(BLOCKS):
        block = h_s[pl.ds(c, 128, stride=8), :]
        hy_ref[:, c * 128 : (c + 1) * 128] = block.astype(BF16)
        turned = block.T
        xt_s[c] = turned.astype(BF16)
        squares = squares + turned * turned
    ss_s[ch] = jnp.broadcast_to(jnp.sum(squares, axis=0, keepdims=True), (8, 128))

    chans = []
    for d in range(1, 4):
        k = lax.rem(ch + d, 4)
        copy = remote(ss_s.at[ch], ss_s.at[ch], sendc.at[d], recvc.at[d], ch=k)
        copy.start()
        chans.append(copy)
    slot = 8 * g + i
    blocks = []
    for d in range(1, 8):
        k = lax.rem(g + d, 8)
        copy = remote(
            xt_s.at[k], xf_ref.at[slot, pl.ds(0, 128), :], senda.at[d], recvx.at[slot], seq=8 * k + i
        )
        copy.start()
        blocks.append(copy)
    xf_ref[slot, 0:128, :] = xt_s[g]
    for copy in chans:
        copy.wait()
    sums = ss_s[0] + ss_s[1] + ss_s[2] + ss_s[3]
    scale = lax.rsqrt(sums / C + EPS)
    high = scale.astype(BF16).astype(F32)
    middle = (scale - high).astype(BF16).astype(F32)
    low = scale - high - middle
    index = lax.broadcasted_iota(jnp.int32, (8, 128), 0)
    packed = jnp.where(index == 0, high, jnp.where(index == 1, middle, low))
    inv_s[...] = jnp.concatenate([packed, jnp.zeros((8, 128), F32)], axis=0).astype(BF16)
    scales = []
    for d in range(1, 8):
        k = lax.rem(g + d, 8)
        copy = remote(
            inv_s, xf_ref.at[slot, pl.ds(128, 16), :], sendi.at[d], recvi.at[d], seq=8 * k + i
        )
        copy.start()
        scales.append(copy)
    xf_ref[slot, 128:144, :] = inv_s[...]

    core = lax.rem(i, 2)
    x = i // 2
    other = 8 * g + 2 * x + 1 - core

    def arrival(b, rows):
        return pltpu.make_async_copy(xf_ref.at[b, rows, :], xf_ref.at[b, rows, :], recvx.at[b])

    passed = []
    for d in range(8):
        k = lax.rem(g + 8 - d, 8)
        b = 8 * k + i
        if d:
            arrival(b, pl.ds(0, 128)).wait()
            scales[d - 1].wait_recv()
        for s in range(1, 4):
            to = 8 * g + 2 * lax.rem(x + s, 4) + core
            copy = remote(xf_ref.at[b], xf_ref.at[b], sendx.at[3 * d + s - 1], recvx.at[b], seq=to)
            copy.start()
            passed.append(copy)
        copy = remote(xf_ref.at[b], xf_ref.at[b], sends.at[4 * d], recvx.at[b], seq=other)
        copy.start()
        passed.append(copy)
    for d in range(8):
        k = lax.rem(g + 8 - d, 8)
        for s in range(1, 4):
            b = 8 * k + 2 * lax.rem(x + 4 - s, 4) + core
            arrival(b, pl.ds(0, SLOT)).wait()
            copy = remote(xf_ref.at[b], xf_ref.at[b], sends.at[4 * d + s], recvx.at[b], seq=other)
            copy.start()
            passed.append(copy)
    for d in range(8):
        k = lax.rem(g + 8 - d, 8)
        for s in range(4):
            b = 8 * k + 2 * lax.rem(x + 4 - s, 4) + 1 - core
            arrival(b, pl.ds(0, SLOT)).wait()
    for copy in blocks + scales + passed:
        copy.wait_send()


def middle_kernel(*refs):
    seq, g, i = here()
    ch = lax.axis_index("ch")
    names = [{"seq": 8 * g + lax.rem(i + d, 8)} for d in range(1, 8)]
    names += [{"seq": 8 * lax.rem(g + d, 8) + i} for d in range(1, 8)]
    names += [{"ch": lax.rem(ch + d, 4)} for d in range(1, 4)]
    greet(names)
    middle_body(*refs)


def attend_body(xf_ref, qg_ref, kg_ref, o_ref, kt_s, vt_s, q_s):
    seq, g, i = here()
    query_gain = qg_ref[pl.ds(g, 1), :]
    key_gain = jnp.broadcast_to(kg_ref[pl.ds(g, 1), :], (128, 128)).T

    def normed(b):
        scale = xf_ref[b, 128:144, :].astype(F32)
        scale = scale[0:1] + (scale[1:2] + scale[2:3])
        return xf_ref[b, 0:128, :].astype(F32) * scale

    def prepare(segment, _):
        for k in range(8):
            rows = normed(8 * segment + k)
            vt_s[segment, :, k * 128 : (k + 1) * 128] = rows.astype(BF16)
            kt_s[segment, :, k * 128 : (k + 1) * 128] = (rows * key_gain).astype(BF16)
        q_s[segment] = (normed(8 * segment + i).T * query_gain).astype(BF16)
        return 0

    lax.fori_loop(0, 8, prepare, 0)
    factor = HEAD ** (-0.5) * math.log2(math.e)
    row = lax.broadcasted_iota(jnp.int32, (128, 1024), 0) + 128 * i
    allowed = lax.broadcasted_iota(jnp.int32, (128, 1024), 1) <= row

    for n in range(8):
        query = q_s[n]

        def tile(segment, carry, diagonal):
            peak, total, blend = carry
            score = jnp.dot(query, kt_s[segment], preferred_element_type=F32) * factor
            if diagonal:
                score = jnp.where(allowed, score, -1e30)
            new_peak = jnp.maximum(peak, jnp.max(score, axis=1, keepdims=True))
            weight = jnp.exp2(score - new_peak)
            shrink = jnp.exp2(peak - new_peak)
            total = total * shrink + jnp.sum(weight, axis=1, keepdims=True)
            blend = blend * shrink + lax.dot_general(
                weight.astype(BF16), vt_s[segment], (((1,), (1,)), ((), ())), preferred_element_type=F32
            )
            return new_peak, total, blend

        carry = (jnp.full((128, 1), -1e30, F32), jnp.zeros((128, 1), F32), jnp.zeros((128, 128), F32))
        carry = tile(n, carry, True)
        if n:
            carry = lax.fori_loop(0, n, lambda s, carry: tile(s, carry, False), carry)
        o_ref[n] = (carry[2] / carry[1]).astype(BF16)


def return_kernel(o_ref, out_ref, send, recv):
    seq, g, i = here()
    greet([{"seq": 8 * lax.rem(g + d, 8) + i} for d in range(1, 8)])
    mine = pl.ds(pl.multiple_of(128 * g, 128), 128)
    copies = []
    for d in range(1, 8):
        k = lax.rem(g + d, 8)
        copy = remote(o_ref.at[k], out_ref.at[:, mine], send.at[d], recv.at[d], seq=8 * k + i)
        copy.start()
        copies.append(copy)
    out_ref[:, mine] = o_ref[g]
    for copy in copies:
        copy.wait()


def vmem(*shape, dtype=F32):
    return pltpu.VMEM(shape, dtype)


def in_vmem(count):
    return [pl.BlockSpec(memory_space=pltpu.VMEM)] * count


def dmas(count):
    return pltpu.SemaphoreType.DMA((count,))


def on_device(
    token_ids, embedding, short_filter, medium_filter, long_residue, long_rate, query_gain, key_gain
):
    seq_count = lax.axis_size("seq")
    lifted = token_ids + 1
    near = lax.ppermute(lifted, "seq", [(k, k + 1) for k in range(seq_count - 1)])
    far = lax.ppermute(lifted, "seq", [(k, k + 2) for k in range(seq_count - 2)])
    tokens = jnp.stack([far, near, lifted]) - 1

    shape = jax.ShapeDtypeStruct
    gated, local, ends, decay = pl.pallas_call(
        front_kernel,
        out_shape=[shape((1024, 128), F32), shape((1024, 128), F32), shape((128, 128), F32), shape((128, 128), F32)],
        in_specs=in_vmem(6),
        out_specs=in_vmem(4),
        scratch_shapes=[vmem(2176, 128), vmem(2048, 128), vmem(64, 128), vmem(1024, 128), vmem(128, 128)],
        compiler_params=pltpu.CompilerParams(vmem_limit_bytes=LIMIT),
        name="front",
    )(tokens, embedding, short_filter, medium_filter, long_residue, long_rate)

    hyena_out, blocks = pl.pallas_call(
        middle_kernel,
        out_shape=[shape((TOK, 1024), BF16), shape((64, SLOT, 128), BF16)],
        in_specs=in_vmem(5),
        out_specs=in_vmem(2),
        scratch_shapes=[
            vmem(128, 128), vmem(128, 128), vmem(128, 128), vmem(128, 128), vmem(16, 128),
            vmem(1024, 128), vmem(8, 128, 128, dtype=BF16), vmem(16, 128, dtype=BF16), vmem(4, 8, 128),
            dmas(8), dmas(8), dmas(8), dmas(8), dmas(8), dmas(8), dmas(4), dmas(4), dmas(8), dmas(8), dmas(8),
            dmas(24), dmas(32), dmas(64),
        ],
        compiler_params=pltpu.CompilerParams(vmem_limit_bytes=LIMIT, collective_id=0, has_side_effects=True),
        name="middle",
    )(long_rate, gated, local, ends, decay)

    blended = pl.pallas_call(
        attend_body,
        out_shape=shape((8, 128, 128), BF16),
        in_specs=in_vmem(3),
        out_specs=in_vmem(1)[0],
        scratch_shapes=[vmem(8, 128, 1024, dtype=BF16), vmem(8, 128, 1024, dtype=BF16), vmem(8, 128, 128, dtype=BF16)],
        compiler_params=pltpu.CompilerParams(vmem_limit_bytes=LIMIT),
        name="attend",
    )(blocks, query_gain.reshape(8, 128), key_gain.reshape(8, 128))

    attended = pl.pallas_call(
        return_kernel,
        out_shape=shape((TOK, 1024), BF16),
        in_specs=in_vmem(1),
        out_specs=in_vmem(1)[0],
        scratch_shapes=[dmas(8), dmas(8)],
        compiler_params=pltpu.CompilerParams(vmem_limit_bytes=LIMIT, collective_id=1, has_side_effects=True),
        name="give_back",
    )(blended)
    return hyena_out, attended


def solution(mesh):
    in_specs = (
        P("seq"),
        P(None, "ch"),
        P(None, "ch"),
        P(None, "ch"),
        P(None, "ch"),
        P(None, "ch"),
        P("ch"),
        P("ch"),
    )
    out_specs = (P("seq", "ch"), P("seq", "ch"))
    return jax.shard_map(
        on_device, mesh=mesh, in_specs=in_specs, out_specs=out_specs, check_vma=False
    )
```

```python
import math

import jax
import jax.numpy as jnp
from jax import lax
from jax.experimental import pallas as pl
from jax.experimental.pallas import tpu as pltpu
from jax.sharding import PartitionSpec as P

C = 4096
HEAD = 128
EPS = 1e-05
TOK = 128
BLOCKS = 8
MESH = pl.DeviceIdType.MESH
F32 = jnp.float32
BF16 = jnp.bfloat16
LIMIT = 60 << 20

OFFSETS = ((0, 0), (1, 0), (3, 0), (2, 0), (0, 1), (1, 1), (3, 1), (2, 1))


def rows_of(step):
    return pl.ds(pl.multiple_of(8 * step, 8), 128)


def part(k):
    return pl.ds(pl.multiple_of(16 * k, 16), 16)


def here():
    seq = lax.axis_index("seq")
    return seq, seq // 8, lax.rem(seq, 8)


def remote(source, target, send, receive, **where):
    return pltpu.make_async_remote_copy(
        src_ref=source, dst_ref=target, send_sem=send, recv_sem=receive, device_id=where, device_id_type=MESH
    )


def landed(ref, semaphore):
    pltpu.make_async_copy(ref, ref, semaphore).wait()


def embed(tokens, emb_ref, e_s, first, keep):
    column = jnp.broadcast_to(tokens.astype(F32), (128, 128)).T[128 - keep :]
    lane = lax.broadcasted_iota(jnp.int32, column.shape, 1).astype(F32)
    one_hot = jnp.concatenate(
        [jnp.where(column == lane + 128.0 * k, 1.0, 0.0).astype(BF16) for k in range(4)], axis=1
    )
    for pair in range(4):
        rows = jnp.dot(one_hot, emb_ref[:, pair * 256 : pair * 256 + 256], preferred_element_type=F32)
        for k in range(2):
            e_s[pl.ds(8 * first + 2 * pair + k, keep, stride=8), :] = rows[:, k * 128 : k * 128 + 128]


def whole_kernel(
    tok_ref, emb_ref, short_ref, med_ref, res_ref, rate_ref, qg_ref, kg_ref, hy_ref, out_ref,
    near_s, far_s, e_s, sg_s, sw_s, mw_s, cf_s, lam_s, mg_s, yl_s, end_s,
    got1, got2, got3, pre_s, group_s, h_s, xt_s, ss_s, inv_s, xf_s, kn_s, vt_s, q_s, o_s,
    sendt, recvt, send1, recv1, send2, recv2, send3, recv3, sendc, recvc, sendi, recvi, sendj, recvj,
    senda, sendx, sendo, recvx, sendr, recvr,
):
    seq, g, i = here()
    ch = lax.axis_index("ch")
    y, half, x, core = g // 2, lax.rem(g, 2), i // 2, lax.rem(i, 2)

    def group_at(dy, dz):
        return 2 * lax.rem(y + dy, 4) + lax.rem(half + dz, 2)

    names = [{"seq": 8 * g + lax.rem(i + d, 8)} for d in range(1, 8)]
    names += [{"seq": 8 * lax.rem(g + d, 8) + i} for d in range(1, 8)]
    names += [{"ch": lax.rem(ch + d, 4)} for d in range(1, 4)]
    names += [{"seq": lax.rem(seq + d, 64)} for d in (1, 2, 62, 63)]
    barrier = pltpu.get_barrier_semaphore()
    for where in names:
        pl.semaphore_signal(barrier, inc=1, device_id=where, device_id_type=MESH)

    for c in range(BLOCKS):
        lanes = slice(c * 128, (c + 1) * 128)
        sw_s[pl.ds(c, 7, stride=8), :] = short_ref[:, lanes]
        mw_s[pl.ds(c, 128, stride=8), :] = med_ref[:, lanes]
        lam_s[pl.ds(c, 16, stride=8), :] = rate_ref[:, lanes]
        cf_s[pl.ds(c, 16, stride=8), :] = res_ref[:, lanes]
    rate = lam_s[...]
    twice = 2.0 * rate
    tail = jnp.ones_like(twice)
    for k in range(9, 1, -1):
        tail = 1.0 - twice * (1.0 / k) * tail
    cf_s[...] = cf_s[...] * jnp.sqrt(twice * tail) * 0.25
    lam_s[...] = jnp.exp(-rate)
    embed(tok_ref[...], emb_ref, e_s, 144, 128)

    pl.semaphore_wait(barrier, len(names))
    tokens = [
        remote(tok_ref, near_s, sendt.at[0], recvt.at[0], seq=lax.rem(seq + 1, 64)),
        remote(tok_ref, far_s, sendt.at[1], recvt.at[1], seq=lax.rem(seq + 2, 64)),
    ]
    for copy in tokens:
        copy.start()

    def short_block(block, _):
        first = 16 + block * 16
        own = e_s[rows_of(first), :].reshape(16, 8, 128)
        total = own * sw_s[0:8, :]
        for j in range(1, 7):
            total = total + e_s[rows_of(first - j), :].reshape(16, 8, 128) * sw_s[8 * j : 8 * j + 8, :]
        gated = (own * total).astype(BF16).astype(F32)
        sg_s[rows_of(16 * block), :] = gated.reshape(128, 128)
        return 0

    lax.fori_loop(9, 16, short_block, 0)
    for copy in tokens:
        copy.wait()
    embed(jnp.where(seq >= 1, near_s[...], -1), emb_ref, e_s, 16, 128)
    embed(jnp.where(seq >= 2, far_s[...], -1), emb_ref, e_s, 0, 16)
    lax.fori_loop(0, 9, short_block, 0)

    def medium_block(block, _):
        def taps(chunk, total):
            base = 128 + 16 * block - 16 * chunk - 15
            window = sg_s[pl.ds(pl.multiple_of(8 * base, 8), 31 * 8), :].reshape(31, 8, 128)
            weight = mw_s[rows_of(16 * chunk), :].reshape(16, 8, 128)
            for j in range(16):
                total = total + weight[j][None] * window[15 - j : 31 - j]
            return total

        total = lax.fori_loop(0, 8, taps, jnp.zeros((16, 8, 128), F32))
        own = sg_s[rows_of(128 + 16 * block), :].reshape(16, 8, 128)
        gated = (own * total).astype(BF16).astype(F32)
        mg_s[rows_of(16 * block), :] = gated.reshape(128, 128)
        return 0

    lax.fori_loop(0, 8, medium_block, 0)

    lam = lam_s[...].reshape(16, 8, 128)
    coef = cf_s[...].reshape(16, 8, 128)

    def tile_of(step):
        return pl.ds(pl.multiple_of(8 * step, 8), 8)

    def forget(block, state):
        for k in range(8):
            state = lam * state + coef * mg_s[tile_of(8 * block + k), :][None]
        return state

    state = lax.fori_loop(0, 16, forget, jnp.zeros((16, 8, 128), F32))
    for r in range(16):
        end_s[pl.ds(r, 8, stride=16), :] = state[r]

    first_scan, second_scan, third_scan = [], [], []
    for d in range(1, 8):
        k = lax.rem(i + d, 8)
        copy = remote(end_s.at[part(k), :], got1.at[part(i), :], send1.at[d], recv1.at[d], seq=8 * g + k)
        copy.start()
        first_scan.append(copy)
    got1[part(i), :] = end_s[part(i), :]

    def local(block, state):
        for k in range(4):
            tile = tile_of(4 * block + k)
            state = lam * state + coef * mg_s[tile, :][None]
            yl_s[tile, :] = jnp.sum(state, axis=0)
        return state

    lax.fori_loop(0, 32, local, jnp.zeros((16, 8, 128), F32))
    rate = rate_ref[:, pl.ds(pl.multiple_of(128 * i, 128), 128)]
    block_decay = jnp.exp(-128.0 * rate)
    group_decay = jnp.exp(-1024.0 * rate)
    for copy in first_scan:
        copy.wait()
    running = jnp.zeros((16, 128), F32)
    for k in range(8):
        pre_s[16 * k : 16 * k + 16, :] = running
        running = block_decay * running + got1[16 * k : 16 * k + 16, :]
    group_s[...] = running
    for d in range(7, 0, -1):
        k = group_at(*OFFSETS[d])
        copy = remote(group_s, got2.at[part(g), :], send2.at[d], recv2.at[d], seq=8 * k + i)
        copy.start()
        second_scan.append(copy)
    got2[part(g), :] = running
    for copy in second_scan:
        copy.wait()
    before = jnp.zeros((16, 128), F32)
    for k in range(8):
        before = jnp.where(k < g, group_decay * before + got2[16 * k : 16 * k + 16, :], before)
    for k in range(8):
        pre_s[16 * k : 16 * k + 16, :] = pre_s[16 * k : 16 * k + 16, :] + before
        before = before * block_decay
    for d in range(1, 8):
        k = lax.rem(i + d, 8)
        copy = remote(pre_s.at[part(k), :], got3.at[part(i), :], send3.at[d], recv3.at[d], seq=8 * g + k)
        copy.start()
        third_scan.append(copy)
    got3[part(i), :] = pre_s[part(i), :]
    for copy in third_scan:
        copy.wait()

    state = jnp.stack([got3[pl.ds(r, 8, stride=16), :] for r in range(16)], axis=0)

    def carried(block, state):
        for k in range(4):
            tile = tile_of(4 * block + k)
            state = lam * state
            full = yl_s[tile, :] + jnp.sum(state, axis=0)
            h_s[tile, :] = (mg_s[tile, :] * full).astype(BF16).astype(F32)
        return state

    lax.fori_loop(0, 32, carried, state)

    squares = jnp.zeros((128, 128), F32)
    for c in range(BLOCKS):
        block = h_s[pl.ds(c, 128, stride=8), :]
        turned = block.T
        xt_s[c] = turned.astype(BF16)
        squares = squares + turned * turned
        hy_ref[:, c * 128 : (c + 1) * 128] = block.astype(BF16)
    ss_s[ch] = jnp.sum(squares, axis=0, keepdims=True)

    sums = []
    for d in range(1, 4):
        k = lax.rem(ch + d, 4)
        copy = remote(ss_s.at[ch], ss_s.at[ch], sendc.at[d], recvc.at[d], ch=k)
        copy.start()
        sums.append(copy)
    slot = 8 * g + i
    sent = []
    for d in range(7, 0, -1):
        k = group_at(*OFFSETS[d])
        copy = remote(xt_s.at[k], xf_s.at[slot], senda.at[d], recvx.at[slot], seq=8 * k + i)
        copy.start()
        sent.append(copy)
    xf_s[slot] = xt_s[g]

    sources = [2 * lax.rem(y + 4 - dy, 4) + lax.rem(half + dz, 2) for dy, dz in OFFSETS]
    places = [8 * k for k in sources]
    right, left = 8 * g + 2 * lax.rem(x + 1, 4) + core, 8 * g + 2 * lax.rem(x + 3, 4) + core
    other = 8 * g + 2 * x + 1 - core

    def along(b, n, semaphores, to):
        copy = remote(xf_s.at[b], xf_s.at[b], semaphores.at[n], recvx.at[b], seq=to)
        copy.start()
        sent.append(copy)

    def own_column(d):
        b = places[d] + i
        if d:
            landed(xf_s.at[b], recvx.at[b])
        along(b, 3 * d, sendx, right)
        along(b, 3 * d + 1, sendx, left)
        along(b, 4 * d, sendo, other)

    def neighbours(d):
        b = places[d] + 2 * lax.rem(x + 3, 4) + core
        landed(xf_s.at[b], recvx.at[b])
        if d % 2 == 0:
            along(b, 3 * d + 2, sendx, right)
        along(b, 4 * d + 1, sendo, other)
        b = places[d] + 2 * lax.rem(x + 1, 4) + core
        landed(xf_s.at[b], recvx.at[b])
        if d % 2 == 1:
            along(b, 3 * d + 2, sendx, left)
        along(b, 4 * d + 2, sendo, other)

    def opposite(d):
        b = places[d] + 2 * lax.rem(x + 2, 4) + core
        landed(xf_s.at[b], recvx.at[b])
        along(b, 4 * d + 3, sendo, other)

    def row_at(i_, g_):
        return 8 * i_ + 4 * lax.rem(g_, 2) + g_ // 2

    def scales_out(z):
        rows = pl.ds(8 * i + 4 * lax.rem(half + z, 2), 4)
        for d in range(4 * z, 4 * z + 4):
            if d:
                landed(inv_s.at[row_at(i, sources[d])], recvi.at[d])
        for d in range(1, 8):
            to = 8 * g + lax.rem(i + d, 8)
            copy = remote(inv_s.at[rows], inv_s.at[rows], sendj.at[8 * z + d], recvj.at[8 * z + d], seq=to)
            copy.start()
            sent.append(copy)

    def scales_in(z):
        for d in range(1, 8):
            rows = pl.ds(8 * lax.rem(i + 8 - d, 8) + 4 * lax.rem(half + z, 2), 4)
            landed(inv_s.at[rows], recvj.at[8 * z + d])

    query_gain = jnp.broadcast_to(qg_ref[pl.ds(g, 1), :], (128, 128)).T
    key_gain = jnp.broadcast_to(kg_ref[pl.ds(g, 1), :], (128, 128)).T

    def normed(b, i_, g_):
        return xf_s[b].astype(F32) * inv_s[row_at(i_, g_)]

    def prepare(d):
        k = sources[d]
        for s in range(4):
            b = places[d] + 2 * lax.rem(x + s, 4) + 1 - core
            landed(xf_s.at[b], recvx.at[b])
        for n in range(8):
            rows = normed(places[d] + n, n, k)
            vt_s[k, :, 128 * n : 128 * n + 128] = rows.astype(BF16)
            kn_s[k, 128 * n : 128 * n + 128, :] = (rows * key_gain).T.astype(BF16)

    own_column(0)
    for copy in sums:
        copy.wait()
    total = ss_s[0] + ss_s[1] + ss_s[2] + ss_s[3]
    inv_s[row_at(i, g)] = lax.rsqrt(total / C + EPS)
    mine = inv_s.at[row_at(i, g)]
    for d in range(7, 0, -1):
        copy = remote(mine, mine, sendi.at[d], recvi.at[d], seq=8 * group_at(*OFFSETS[d]) + i)
        copy.start()
        sent.append(copy)
    own_column(1)
    own_column(2)
    neighbours(0)
    own_column(3)
    neighbours(1)
    opposite(0)
    scales_out(0)
    neighbours(2)
    opposite(1)
    neighbours(3)
    own_column(4)
    opposite(2)
    own_column(5)
    neighbours(4)
    opposite(3)
    own_column(6)
    neighbours(5)
    own_column(7)
    scales_out(1)
    opposite(4)
    neighbours(6)
    scales_in(0)
    prepare(0)
    opposite(5)
    neighbours(7)
    prepare(1)
    opposite(6)
    prepare(2)
    opposite(7)
    prepare(3)
    for n in range(8):
        q_s[:, 128 * n : 128 * n + 128] = (normed(8 * n + i, i, n) * query_gain).astype(BF16)
    scales_in(1)
    for d in range(4, 8):
        prepare(d)

    factor = HEAD ** (-0.5) * math.log2(math.e)
    column = lax.broadcasted_iota(jnp.int32, (1024, 128), 1) + 128 * i
    allowed = lax.broadcasted_iota(jnp.int32, (1024, 128), 0) <= column

    def attend(n, segment, carry, diagonal):
        peak, total, blend = carry
        score = jnp.dot(kn_s[segment], q_s[:, 128 * n : 128 * n + 128], preferred_element_type=F32) * factor
        if diagonal:
            score = jnp.where(allowed, score, -1e30)
        new_peak = jnp.maximum(peak, jnp.max(score, axis=0, keepdims=True))
        weight = jnp.exp2(score - new_peak)
        shrink = jnp.exp2(peak - new_peak)
        total = total * shrink + jnp.sum(weight, axis=0, keepdims=True)
        blend = blend * shrink + jnp.dot(vt_s[segment], weight.astype(BF16), preferred_element_type=F32)
        return new_peak, total, blend

    columns = pl.ds(pl.multiple_of(128 * g, 128), 128)
    given = [
        remote(o_s.at[n], out_ref.at[:, columns], sendr.at[n], recvr.at[g], seq=8 * n + i) for n in range(8)
    ]
    for base in (4, 0):
        carries = [
            (jnp.full((1, 128), -1e30, F32), jnp.zeros((1, 128), F32), jnp.zeros((128, 128), F32))
            for _ in range(4)
        ]
        for segment in range(base, base + 4):
            for n in range(segment, base + 4):
                carries[n - base] = attend(n, segment, carries[n - base], n == segment)
        if base:
            carries = lax.fori_loop(
                0, base, lambda s, held: [attend(base + n, s, held[n], False) for n in range(4)], carries
            )
        for n in range(4):
            o_s[base + n] = (carries[n][2] / carries[n][1]).T.astype(BF16)
        for n in range(base, base + 4):
            pl.when(g != n)(given[n].start)
    out_ref[:, columns] = o_s[g]
    for n in range(8):

        @pl.when(g != n)
        def _(n=n):
            landed(out_ref.at[:, pl.ds(128 * n, 128)], recvr.at[n])
            given[n].wait_send()

    for copy in sent:
        copy.wait_send()


def vmem(*shape, dtype=F32):
    return pltpu.VMEM(shape, dtype)


def in_vmem(count):
    return [pl.BlockSpec(memory_space=pltpu.VMEM)] * count


def dmas(count):
    return pltpu.SemaphoreType.DMA((count,))


def on_device(
    token_ids, embedding, short_filter, medium_filter, long_residue, long_rate, query_gain, key_gain
):
    shape = jax.ShapeDtypeStruct
    counts = (2, 2, 8, 8, 8, 8, 8, 8, 4, 4, 8, 8, 16, 16, 8, 24, 32, 64, 8, 8)
    return pl.pallas_call(
        whole_kernel,
        out_shape=[shape((TOK, 1024), BF16), shape((TOK, 1024), BF16)],
        in_specs=in_vmem(8),
        out_specs=in_vmem(2),
        scratch_shapes=[
            vmem(1, 128, dtype=jnp.int32), vmem(1, 128, dtype=jnp.int32),
            vmem(2176, 128), vmem(2048, 128), vmem(64, 128), vmem(1024, 128), vmem(128, 128), vmem(128, 128),
            vmem(1024, 128), vmem(1024, 128), vmem(128, 128),
            vmem(128, 128), vmem(128, 128), vmem(128, 128), vmem(128, 128), vmem(16, 128),
            vmem(1024, 128), vmem(8, 128, 128, dtype=BF16), vmem(4, 1, 128), vmem(64, 1, 128),
            vmem(64, 128, 128, dtype=BF16), vmem(8, 1024, 128, dtype=BF16), vmem(8, 128, 1024, dtype=BF16),
            vmem(128, 1024, dtype=BF16), vmem(8, 128, 128, dtype=BF16),
        ]
        + [dmas(count) for count in counts],
        compiler_params=pltpu.CompilerParams(vmem_limit_bytes=LIMIT, collective_id=0, has_side_effects=True),
        name="whole",
    )(
        token_ids.reshape(1, TOK), embedding, short_filter, medium_filter, long_residue, long_rate,
        query_gain.reshape(8, 128), key_gain.reshape(8, 128),
    )


def solution(mesh):
    in_specs = (
        P("seq"),
        P(None, "ch"),
        P(None, "ch"),
        P(None, "ch"),
        P(None, "ch"),
        P(None, "ch"),
        P("ch"),
        P("ch"),
    )
    out_specs = (P("seq", "ch"), P("seq", "ch"))
    return jax.shard_map(
        on_device, mesh=mesh, in_specs=in_specs, out_specs=out_specs, check_vma=False
    )
```

```python
import math

import jax
import jax.numpy as jnp
from jax import lax
from jax.experimental import pallas as pl
from jax.experimental.pallas import tpu as pltpu
from jax.sharding import PartitionSpec as P

C = 4096
HEAD = 128
EPS = 1e-05
TOK = 128
BLOCKS = 8
MESH = pl.DeviceIdType.MESH
F32 = jnp.float32
BF16 = jnp.bfloat16
LIMIT = 60 << 20

OFFSETS = ((0, 0), (1, 0), (3, 0), (2, 0), (0, 1), (1, 1), (3, 1), (2, 1))


def rows_of(step):
    return pl.ds(pl.multiple_of(8 * step, 8), 128)


def part(k):
    return pl.ds(pl.multiple_of(16 * k, 16), 16)


def here():
    seq = lax.axis_index("seq")
    return seq, seq // 8, lax.rem(seq, 8)


def remote(source, target, send, receive, **where):
    return pltpu.make_async_remote_copy(
        src_ref=source, dst_ref=target, send_sem=send, recv_sem=receive, device_id=where, device_id_type=MESH
    )


def landed(ref, semaphore):
    pltpu.make_async_copy(ref, ref, semaphore).wait()


def embed(tokens, emb_ref, e_s, first, keep):
    column = jnp.broadcast_to(tokens.astype(F32), (128, 128)).T[128 - keep :]
    lane = lax.broadcasted_iota(jnp.int32, column.shape, 1).astype(F32)
    one_hot = jnp.concatenate(
        [jnp.where(column == lane + 128.0 * k, 1.0, 0.0).astype(BF16) for k in range(4)], axis=1
    )
    for pair in range(4):
        rows = jnp.dot(one_hot, emb_ref[:, pair * 256 : pair * 256 + 256], preferred_element_type=F32)
        for k in range(2):
            e_s[pl.ds(8 * first + 2 * pair + k, keep, stride=8), :] = rows[:, k * 128 : k * 128 + 128]


def whole_kernel(
    tok_ref, emb_in, short_in, med_in, res_in, rate_in, qg_ref, kg_ref, hy_ref, out_ref,
    emb_ref, short_ref, med_ref, res_ref, rate_ref, fetch,
    near_s, far_s, e_s, sg_s, sw_s, mw_s, cf_s, lam_s, mg_s, yl_s, end_s,
    got1, got2, got3, pre_s, group_s, h_s, xt_s, ss_s, inv_s, xf_s, kn_s, vt_s, q_s, o_s,
    peak_s, total_s, blend_s,
    sendt, recvt, send1, recv1, send2, recv2, send3, recv3, sendc, recvc, sendi, recvi, sendj, recvj,
    senda, sendx, sendo, recvx, sendr, recvr,
):
    seq, g, i = here()
    ch = lax.axis_index("ch")
    y, half, x, core = g // 2, lax.rem(g, 2), i // 2, lax.rem(i, 2)

    def group_at(dy, dz):
        return 2 * lax.rem(y + dy, 4) + lax.rem(half + dz, 2)

    names = [{"seq": 8 * g + lax.rem(i + d, 8)} for d in range(1, 8)]
    names += [{"seq": 8 * lax.rem(g + d, 8) + i} for d in range(1, 8)]
    names += [{"ch": lax.rem(ch + d, 4)} for d in range(1, 4)]
    names += [{"seq": lax.rem(seq + d, 64)} for d in (1, 2, 62, 63)]
    barrier = pltpu.get_barrier_semaphore()
    for where in names:
        pl.semaphore_signal(barrier, inc=1, device_id=where, device_id_type=MESH)

    fetches = [
        pltpu.make_async_copy(source, target, fetch.at[n])
        for n, (source, target) in enumerate(
            [(rate_in, rate_ref), (res_in, res_ref), (short_in, short_ref), (med_in, med_ref), (emb_in, emb_ref)]
        )
    ]
    for copy in fetches:
        copy.start()
    for copy in fetches:
        copy.wait()

    for c in range(BLOCKS):
        lanes = slice(c * 128, (c + 1) * 128)
        sw_s[pl.ds(c, 7, stride=8), :] = short_ref[:, lanes]
        mw_s[pl.ds(c, 128, stride=8), :] = med_ref[:, lanes]
        lam_s[pl.ds(c, 16, stride=8), :] = rate_ref[:, lanes]
        cf_s[pl.ds(c, 16, stride=8), :] = res_ref[:, lanes]
    rate = lam_s[...]
    twice = 2.0 * rate
    tail = jnp.ones_like(twice)
    for k in range(9, 1, -1):
        tail = 1.0 - twice * (1.0 / k) * tail
    cf_s[...] = cf_s[...] * jnp.sqrt(twice * tail) * 0.25
    lam_s[...] = jnp.exp(-rate)
    embed(tok_ref[...], emb_ref, e_s, 144, 128)

    pl.semaphore_wait(barrier, len(names))
    tokens = [
        remote(tok_ref, near_s, sendt.at[0], recvt.at[0], seq=lax.rem(seq + 1, 64)),
        remote(tok_ref, far_s, sendt.at[1], recvt.at[1], seq=lax.rem(seq + 2, 64)),
    ]
    for copy in tokens:
        copy.start()

    def short_block(block, _):
        first = 16 + block * 16
        own = e_s[rows_of(first), :].reshape(16, 8, 128)
        total = own * sw_s[0:8, :]
        for j in range(1, 7):
            total = total + e_s[rows_of(first - j), :].reshape(16, 8, 128) * sw_s[8 * j : 8 * j + 8, :]
        gated = (own * total).astype(BF16).astype(F32)
        sg_s[rows_of(16 * block), :] = gated.reshape(128, 128)
        return 0

    lax.fori_loop(9, 16, short_block, 0)

    def taps_of(block):
        def taps(chunk, total):
            base = 128 + 16 * block - 16 * chunk - 15
            window = sg_s[pl.ds(pl.multiple_of(8 * base, 8), 31 * 8), :].reshape(31, 8, 128)
            weight = mw_s[rows_of(16 * chunk), :].reshape(16, 8, 128)
            for j in range(16):
                total = total + weight[j][None] * window[15 - j : 31 - j]
            return total

        return taps

    def medium_start(block, _):
        total = lax.fori_loop(0, block - 1, taps_of(block), jnp.zeros((16, 8, 128), F32))
        mg_s[rows_of(16 * block), :] = total.reshape(128, 128)
        return 0

    mg_s[0:256, :] = jnp.zeros((256, 128), F32)
    lax.fori_loop(2, 8, medium_start, 0)
    for copy in tokens:
        copy.wait()
    embed(jnp.where(seq >= 1, near_s[...], -1), emb_ref, e_s, 16, 128)
    embed(jnp.where(seq >= 2, far_s[...], -1), emb_ref, e_s, 0, 16)
    lax.fori_loop(0, 9, short_block, 0)

    def medium_block(block, _):
        total = mg_s[rows_of(16 * block), :].reshape(16, 8, 128)
        total = lax.fori_loop(jnp.maximum(block - 1, 0), 8, taps_of(block), total)
        own = sg_s[rows_of(128 + 16 * block), :].reshape(16, 8, 128)
        gated = (own * total).astype(BF16).astype(F32)
        mg_s[rows_of(16 * block), :] = gated.reshape(128, 128)
        return 0

    lax.fori_loop(0, 8, medium_block, 0)

    lam = lam_s[...].reshape(16, 8, 128)
    coef = cf_s[...].reshape(16, 8, 128)

    def tile_of(step):
        return pl.ds(pl.multiple_of(8 * step, 8), 8)

    def forget(block, state):
        for k in range(8):
            state = lam * state + coef * mg_s[tile_of(8 * block + k), :][None]
        return state

    state = lax.fori_loop(0, 16, forget, jnp.zeros((16, 8, 128), F32))
    for r in range(16):
        end_s[pl.ds(r, 8, stride=16), :] = state[r]

    first_scan, second_scan, third_scan = [], [], []
    for d in range(1, 8):
        k = lax.rem(i + d, 8)
        copy = remote(end_s.at[part(k), :], got1.at[part(i), :], send1.at[d], recv1.at[d], seq=8 * g + k)
        copy.start()
        first_scan.append(copy)
    got1[part(i), :] = end_s[part(i), :]

    def local(block, state):
        for k in range(4):
            tile = tile_of(4 * block + k)
            state = lam * state + coef * mg_s[tile, :][None]
            yl_s[tile, :] = jnp.sum(state, axis=0)
        return state

    lax.fori_loop(0, 32, local, jnp.zeros((16, 8, 128), F32))
    rate = rate_ref[:, pl.ds(pl.multiple_of(128 * i, 128), 128)]
    block_decay = jnp.exp(-128.0 * rate)
    group_decay = jnp.exp(-1024.0 * rate)
    for copy in first_scan:
        copy.wait()
    running = jnp.zeros((16, 128), F32)
    for k in range(8):
        pre_s[16 * k : 16 * k + 16, :] = running
        running = block_decay * running + got1[16 * k : 16 * k + 16, :]
    group_s[...] = running
    for d in range(7, 0, -1):
        k = group_at(*OFFSETS[d])
        copy = remote(group_s, got2.at[part(g), :], send2.at[d], recv2.at[d], seq=8 * k + i)
        copy.start()
        second_scan.append(copy)
    got2[part(g), :] = running
    for copy in second_scan:
        copy.wait()
    before = jnp.zeros((16, 128), F32)
    for k in range(8):
        before = jnp.where(k < g, group_decay * before + got2[16 * k : 16 * k + 16, :], before)
    for k in range(8):
        pre_s[16 * k : 16 * k + 16, :] = pre_s[16 * k : 16 * k + 16, :] + before
        before = before * block_decay
    for d in range(1, 8):
        k = lax.rem(i + d, 8)
        copy = remote(pre_s.at[part(k), :], got3.at[part(i), :], send3.at[d], recv3.at[d], seq=8 * g + k)
        copy.start()
        third_scan.append(copy)
    got3[part(i), :] = pre_s[part(i), :]
    for copy in third_scan:
        copy.wait()

    state = jnp.stack([got3[pl.ds(r, 8, stride=16), :] for r in range(16)], axis=0)

    def carried(block, state):
        for k in range(4):
            tile = tile_of(4 * block + k)
            state = lam * state
            full = yl_s[tile, :] + jnp.sum(state, axis=0)
            h_s[tile, :] = (mg_s[tile, :] * full).astype(BF16).astype(F32)
        return state

    lax.fori_loop(0, 32, carried, state)

    squares = jnp.zeros((128, 128), F32)
    for c in range(BLOCKS):
        block = h_s[pl.ds(c, 128, stride=8), :]
        turned = block.T
        xt_s[c] = turned.astype(BF16)
        squares = squares + turned * turned
        hy_ref[:, c * 128 : (c + 1) * 128] = block.astype(BF16)
    ss_s[ch] = jnp.sum(squares, axis=0, keepdims=True)

    sums = []
    for d in range(1, 4):
        k = lax.rem(ch + d, 4)
        copy = remote(ss_s.at[ch], ss_s.at[ch], sendc.at[d], recvc.at[d], ch=k)
        copy.start()
        sums.append(copy)
    slot = 8 * g + i
    sent = []
    for d in range(7, 0, -1):
        k = group_at(*OFFSETS[d])
        copy = remote(xt_s.at[k], xf_s.at[slot], senda.at[d], recvx.at[slot], seq=8 * k + i)
        copy.start()
        sent.append(copy)
    xf_s[slot] = xt_s[g]

    sources = [2 * lax.rem(y + 4 - dy, 4) + lax.rem(half + dz, 2) for dy, dz in OFFSETS]
    places = [8 * k for k in sources]
    other = 8 * g + 2 * x + 1 - core

    def along(b, n, semaphores, to):
        copy = remote(xf_s.at[b], xf_s.at[b], semaphores.at[n], recvx.at[b], seq=to)
        copy.start()
        sent.append(copy)

    def own_column(d):
        b = places[d] + i
        if d:
            landed(xf_s.at[b], recvx.at[b])
        for s in range(1, 4):
            along(b, 3 * d + s - 1, sendx, 8 * g + 2 * lax.rem(x + s, 4) + core)
        along(b, 4 * d, sendo, other)

    def from_x(d):
        for s in (1, 3, 2):
            b = places[d] + 2 * lax.rem(x + s, 4) + core
            landed(xf_s.at[b], recvx.at[b])
            along(b, 4 * d + s, sendo, other)

    def row_at(i_, g_):
        return 8 * i_ + 4 * lax.rem(g_, 2) + g_ // 2

    def scales_out(z):
        rows = pl.ds(8 * i + 4 * lax.rem(half + z, 2), 4)
        for d in range(4 * z, 4 * z + 4):
            if d:
                landed(inv_s.at[row_at(i, sources[d])], recvi.at[d])
        for d in range(1, 8):
            to = 8 * g + lax.rem(i + d, 8)
            copy = remote(inv_s.at[rows], inv_s.at[rows], sendj.at[8 * z + d], recvj.at[8 * z + d], seq=to)
            copy.start()
            sent.append(copy)

    def scales_in(z):
        for d in range(1, 8):
            rows = pl.ds(8 * lax.rem(i + 8 - d, 8) + 4 * lax.rem(half + z, 2), 4)
            landed(inv_s.at[rows], recvj.at[8 * z + d])

    query_gain = jnp.broadcast_to(qg_ref[pl.ds(g, 1), :], (128, 128)).T
    key_gain = jnp.broadcast_to(kg_ref[pl.ds(g, 1), :], (128, 128)).T

    def normed(b, i_, g_):
        return xf_s[b].astype(F32) * inv_s[row_at(i_, g_)]

    def prepare(d):
        k = sources[d]
        for s in range(4):
            b = places[d] + 2 * lax.rem(x + s, 4) + 1 - core
            landed(xf_s.at[b], recvx.at[b])
        for n in range(8):
            rows = normed(places[d] + n, n, k)
            vt_s[k, :, 128 * n : 128 * n + 128] = rows.astype(BF16)
            kn_s[k, 128 * n : 128 * n + 128, :] = (rows * key_gain).T.astype(BF16)

    own_column(0)
    for copy in sums:
        copy.wait()
    total = ss_s[0] + ss_s[1] + ss_s[2] + ss_s[3]
    inv_s[row_at(i, g)] = lax.rsqrt(total / C + EPS)
    mine = inv_s.at[row_at(i, g)]
    for d in range(7, 0, -1):
        copy = remote(mine, mine, sendi.at[d], recvi.at[d], seq=8 * group_at(*OFFSETS[d]) + i)
        copy.start()
        sent.append(copy)
    for d in range(1, 4):
        own_column(d)
    scales_out(0)
    for d in range(4, 8):
        own_column(d)
    scales_out(1)
    for d in range(4):
        from_x(d)
    scales_in(0)
    for d in range(4):
        prepare(d)
    for n in range(8):
        q_s[:, 128 * n : 128 * n + 128] = (normed(8 * n + i, i, n) * query_gain).astype(BF16)

    factor = HEAD ** (-0.5) * math.log2(math.e)
    ahead = lax.broadcasted_iota(jnp.int32, (1024, 128), 0) - lax.broadcasted_iota(jnp.int32, (1024, 128), 1)

    def attend(n, segment, carry, masked):
        peak, total, blend = carry
        query = q_s[:, pl.ds(pl.multiple_of(128 * n, 128), 128)]
        score = jnp.dot(kn_s[segment], query, preferred_element_type=F32) * factor
        if masked:
            score = jnp.where(ahead <= 128 * i + 1024 * (n - segment), score, -1e30)
        new_peak = jnp.maximum(peak, jnp.max(score, axis=0, keepdims=True))
        weight = jnp.exp2(score - new_peak)
        shrink = jnp.exp2(peak - new_peak)
        total = total * shrink + jnp.sum(weight, axis=0, keepdims=True)
        blend = blend * shrink + jnp.dot(vt_s[segment], weight.astype(BF16), preferred_element_type=F32)
        return new_peak, total, blend

    def sweep(queries, segments, carries):
        for j in range(4):
            for m in range(3, j - 1, -1):
                carries[m] = attend(2 * m + queries, 2 * j + segments, carries[m], m == j)
        return carries

    for far in (1, 0):
        carries = [
            (jnp.full((1, 128), -1e30, F32), jnp.zeros((1, 128), F32), jnp.zeros((128, 128), F32))
            for _ in range(4)
        ]
        carries = sweep(lax.rem(half + far, 2), half, carries)
        for m in range(4):
            peak_s[4 * far + m], total_s[4 * far + m], blend_s[4 * far + m] = carries[m]
        from_x(4 + 2 * (1 - far))
        from_x(5 + 2 * (1 - far))
    scales_in(1)
    for d in range(4, 8):
        prepare(d)

    columns = pl.ds(pl.multiple_of(128 * g, 128), 128)

    def given(m, far):
        n = 2 * m + lax.rem(half + far, 2)
        place = 4 * far + m
        return remote(o_s.at[place], out_ref.at[:, columns], sendr.at[place], recvr.at[g], seq=8 * n + i)

    for far in (1, 0):
        carries = [(peak_s[4 * far + m], total_s[4 * far + m], blend_s[4 * far + m]) for m in range(4)]
        carries = sweep(lax.rem(half + far, 2), 1 - half, carries)
        for m in range(4):
            o_s[4 * far + m] = (carries[m][2] / carries[m][1]).T.astype(BF16)
        for m in range(4):
            if far:
                given(m, far).start()
            else:
                pl.when(y != m)(given(m, far).start)
    out_ref[:, columns] = o_s[y]
    for n in range(8):

        @pl.when(g != n)
        def _(n=n):
            landed(out_ref.at[:, pl.ds(128 * n, 128)], recvr.at[n])

    for m in range(4):
        given(m, 1).wait_send()
        pl.when(y != m)(given(m, 0).wait_send)
    for copy in sent:
        copy.wait_send()


def finish_kernel(hy_in, out_in, hy_ref, out_ref, semaphores):
    copies = [
        pltpu.make_async_copy(hy_in, hy_ref, semaphores.at[0]),
        pltpu.make_async_copy(out_in, out_ref, semaphores.at[1]),
    ]
    for copy in copies:
        copy.start()
    for copy in copies:
        copy.wait()


def vmem(*shape, dtype=F32):
    return pltpu.VMEM(shape, dtype)


def in_vmem(count):
    return [pl.BlockSpec(memory_space=pltpu.VMEM)] * count


def dmas(count):
    return pltpu.SemaphoreType.DMA((count,))


def on_device(
    token_ids, embedding, short_filter, medium_filter, long_residue, long_rate, query_gain, key_gain
):
    shape = jax.ShapeDtypeStruct
    counts = (2, 2, 8, 8, 8, 8, 8, 8, 4, 4, 8, 8, 16, 16, 8, 24, 32, 64, 8, 8)
    results = pl.pallas_call(
        whole_kernel,
        out_shape=[shape((TOK, 1024), BF16), shape((TOK, 1024), BF16)],
        in_specs=in_vmem(1) + [pl.BlockSpec(memory_space=pl.ANY)] * 5 + in_vmem(2),
        out_specs=in_vmem(2),
        scratch_shapes=[
            vmem(512, 1024, dtype=BF16), vmem(7, 1024), vmem(128, 1024), vmem(16, 1024), vmem(16, 1024), dmas(5),
            vmem(1, 128, dtype=jnp.int32), vmem(1, 128, dtype=jnp.int32),
            vmem(2176, 128), vmem(2048, 128), vmem(64, 128), vmem(1024, 128), vmem(128, 128), vmem(128, 128),
            vmem(1024, 128), vmem(1024, 128), vmem(128, 128),
            vmem(128, 128), vmem(128, 128), vmem(128, 128), vmem(128, 128), vmem(16, 128),
            vmem(1024, 128), vmem(8, 128, 128, dtype=BF16), vmem(4, 1, 128), vmem(64, 1, 128),
            vmem(64, 128, 128, dtype=BF16), vmem(8, 1024, 128, dtype=BF16), vmem(8, 128, 1024, dtype=BF16),
            vmem(128, 1024, dtype=BF16), vmem(8, 128, 128, dtype=BF16),
            vmem(8, 1, 128), vmem(8, 1, 128), vmem(8, 128, 128),
        ]
        + [dmas(count) for count in counts],
        compiler_params=pltpu.CompilerParams(vmem_limit_bytes=LIMIT, collective_id=0, has_side_effects=True),
        name="whole",
    )(
        token_ids.reshape(1, TOK), embedding, short_filter, medium_filter, long_residue, long_rate,
        query_gain.reshape(8, 128), key_gain.reshape(8, 128),
    )
    return pl.pallas_call(
        finish_kernel,
        out_shape=[shape((TOK, 1024), BF16), shape((TOK, 1024), BF16)],
        in_specs=[pl.BlockSpec(memory_space=pl.ANY)] * 2,
        out_specs=in_vmem(2),
        scratch_shapes=[dmas(2)],
        name="finish",
    )(*results)


def solution(mesh):
    in_specs = (
        P("seq"),
        P(None, "ch"),
        P(None, "ch"),
        P(None, "ch"),
        P(None, "ch"),
        P(None, "ch"),
        P("ch"),
        P("ch"),
    )
    out_specs = (P("seq", "ch"), P("seq", "ch"))
    return jax.shard_map(
        on_device, mesh=mesh, in_specs=in_specs, out_specs=out_specs, check_vma=False
    )
```

```python
import math

import jax
import jax.numpy as jnp
from jax import lax
from jax.experimental import pallas as pl
from jax.experimental.pallas import tpu as pltpu
from jax.sharding import PartitionSpec as P

C = 4096
HEAD = 128
EPS = 1e-05
TOK = 128
BLOCKS = 8
MESH = pl.DeviceIdType.MESH
F32 = jnp.float32
BF16 = jnp.bfloat16
LIMIT = 60 << 20

OFFSETS = ((0, 0), (1, 0), (3, 0), (2, 0), (0, 1), (1, 1), (3, 1), (2, 1))


def rows_of(step):
    return pl.ds(pl.multiple_of(8 * step, 8), 128)


def part(k):
    return pl.ds(pl.multiple_of(16 * k, 16), 16)


def here():
    seq = lax.axis_index("seq")
    return seq, seq // 8, lax.rem(seq, 8)


def remote(source, target, send, receive, **where):
    return pltpu.make_async_remote_copy(
        src_ref=source, dst_ref=target, send_sem=send, recv_sem=receive, device_id=where, device_id_type=MESH
    )


def landed(ref, semaphore):
    pltpu.make_async_copy(ref, ref, semaphore).wait()


def embed(tokens, emb_ref, e_s, first, keep):
    column = jnp.broadcast_to(tokens.astype(F32), (128, 128)).T[128 - keep :]
    lane = lax.broadcasted_iota(jnp.int32, column.shape, 1).astype(F32)
    one_hot = jnp.concatenate(
        [jnp.where(column == lane + 128.0 * k, 1.0, 0.0).astype(BF16) for k in range(4)], axis=1
    )
    for pair in range(4):
        rows = jnp.dot(one_hot, emb_ref[:, pair * 256 : pair * 256 + 256], preferred_element_type=F32)
        for k in range(2):
            e_s[pl.ds(8 * first + 2 * pair + k, keep, stride=8), :] = rows[:, k * 128 : k * 128 + 128]


def whole_kernel(
    tok_ref, emb_in, short_in, med_in, res_in, rate_in, qg_ref, kg_ref, hy_ref, out_ref,
    emb_ref, short_ref, med_ref, res_ref, rate_ref, fetch,
    near_s, far_s, e_s, sg_s, sw_s, mw_s, cf_s, lam_s, mg_s, yl_s, end_s,
    got1, got2, got3, pre_s, group_s, h_s, xt_s, ss_s, inv_s, xf_s, kn_s, vt_s, q_s, o_s,
    peak_s, total_s, blend_s,
    sendt, recvt, send1, recv1, send2, recv2, send3, recv3, sendc, recvc, sendi, recvi, sendj, recvj,
    senda, sendx, recva, recvb, recvo, sendr, recvr,
):
    seq, g, i = here()
    ch = lax.axis_index("ch")
    y, half, x, core = g // 2, lax.rem(g, 2), i // 2, lax.rem(i, 2)

    def group_at(dy, dz):
        return 2 * lax.rem(y + dy, 4) + lax.rem(half + dz, 2)

    names = [{"seq": 8 * g + lax.rem(i + d, 8)} for d in range(1, 8)]
    names += [{"seq": 8 * lax.rem(g + d, 8) + i} for d in range(1, 8)]
    names += [{"ch": lax.rem(ch + d, 4)} for d in range(1, 4)]
    names += [{"seq": lax.rem(seq + d, 64)} for d in (1, 2, 62, 63)]
    barrier = pltpu.get_barrier_semaphore()
    for where in names:
        pl.semaphore_signal(barrier, inc=1, device_id=where, device_id_type=MESH)

    fetches = [
        pltpu.make_async_copy(source, target, fetch.at[n])
        for n, (source, target) in enumerate(
            [(rate_in, rate_ref), (res_in, res_ref), (short_in, short_ref), (med_in, med_ref), (emb_in, emb_ref)]
        )
    ]
    for copy in fetches:
        copy.start()
    pl.semaphore_wait(barrier, len(names))
    tokens = [
        remote(tok_ref, near_s, sendt.at[0], recvt.at[0], seq=lax.rem(seq + 1, 64)),
        remote(tok_ref, far_s, sendt.at[1], recvt.at[1], seq=lax.rem(seq + 2, 64)),
    ]
    for copy in tokens:
        copy.start()
    for copy in fetches:
        copy.wait()

    for c in range(BLOCKS):
        lanes = slice(c * 128, (c + 1) * 128)
        sw_s[pl.ds(c, 7, stride=8), :] = short_ref[:, lanes]
        mw_s[pl.ds(c, 128, stride=8), :] = med_ref[:, lanes]
        lam_s[pl.ds(c, 16, stride=8), :] = rate_ref[:, lanes]
        cf_s[pl.ds(c, 16, stride=8), :] = res_ref[:, lanes]
    rate = lam_s[...]
    twice = 2.0 * rate
    tail = jnp.ones_like(twice)
    for k in range(9, 1, -1):
        tail = 1.0 - twice * (1.0 / k) * tail
    cf_s[...] = cf_s[...] * jnp.sqrt(twice * tail) * 0.25
    lam_s[...] = jnp.exp(-rate)
    embed(tok_ref[...], emb_ref, e_s, 144, 128)

    def short_block(block, _):
        first = 16 + block * 16
        own = e_s[rows_of(first), :].reshape(16, 8, 128)
        total = own * sw_s[0:8, :]
        for j in range(1, 7):
            total = total + e_s[rows_of(first - j), :].reshape(16, 8, 128) * sw_s[8 * j : 8 * j + 8, :]
        gated = (own * total).astype(BF16).astype(F32)
        sg_s[rows_of(16 * block), :] = gated.reshape(128, 128)
        return 0

    lax.fori_loop(9, 16, short_block, 0)

    def taps_of(block):
        def taps(chunk, total):
            base = 128 + 16 * block - 16 * chunk - 15
            window = sg_s[pl.ds(pl.multiple_of(8 * base, 8), 31 * 8), :].reshape(31, 8, 128)
            weight = mw_s[rows_of(16 * chunk), :].reshape(16, 8, 128)
            for j in range(16):
                total = total + weight[j][None] * window[15 - j : 31 - j]
            return total

        return taps

    def medium_start(block, _):
        total = lax.fori_loop(0, block - 1, taps_of(block), jnp.zeros((16, 8, 128), F32))
        mg_s[rows_of(16 * block), :] = total.reshape(128, 128)
        return 0

    mg_s[0:256, :] = jnp.zeros((256, 128), F32)
    lax.fori_loop(2, 8, medium_start, 0)
    for copy in tokens:
        copy.wait()
    embed(jnp.where(seq >= 1, near_s[...], -1), emb_ref, e_s, 16, 128)
    embed(jnp.where(seq >= 2, far_s[...], -1), emb_ref, e_s, 0, 16)
    lax.fori_loop(0, 9, short_block, 0)

    def medium_block(block, _):
        total = mg_s[rows_of(16 * block), :].reshape(16, 8, 128)
        total = lax.fori_loop(jnp.maximum(block - 1, 0), 8, taps_of(block), total)
        own = sg_s[rows_of(128 + 16 * block), :].reshape(16, 8, 128)
        gated = (own * total).astype(BF16).astype(F32)
        mg_s[rows_of(16 * block), :] = gated.reshape(128, 128)
        return 0

    lax.fori_loop(0, 8, medium_block, 0)

    lam = lam_s[...].reshape(16, 8, 128)
    coef = cf_s[...].reshape(16, 8, 128)

    def tile_of(step):
        return pl.ds(pl.multiple_of(8 * step, 8), 8)

    def forget(block, state):
        for k in range(8):
            state = lam * state + coef * mg_s[tile_of(8 * block + k), :][None]
        return state

    state = lax.fori_loop(0, 16, forget, jnp.zeros((16, 8, 128), F32))
    for r in range(16):
        end_s[pl.ds(r, 8, stride=16), :] = state[r]

    seven = pl.ds(0, 112)
    for d in range(1, 8):
        k = lax.rem(i + d, 8)
        copy = remote(end_s.at[part(k), :], got1.at[part(i), :], send1.at[0], recv1.at[0], seq=8 * g + k)
        copy.start()
    got1[part(i), :] = end_s[part(i), :]

    def local(block, state):
        for k in range(4):
            tile = tile_of(4 * block + k)
            state = lam * state + coef * mg_s[tile, :][None]
            yl_s[tile, :] = jnp.sum(state, axis=0)
        return state

    lax.fori_loop(0, 32, local, jnp.zeros((16, 8, 128), F32))
    rate = rate_ref[:, pl.ds(pl.multiple_of(128 * i, 128), 128)]
    block_decay = jnp.exp(-128.0 * rate)
    group_decay = jnp.exp(-1024.0 * rate)
    landed(got1.at[seven, :], send1.at[0])
    landed(got1.at[seven, :], recv1.at[0])
    running = jnp.zeros((16, 128), F32)
    for k in range(8):
        pre_s[16 * k : 16 * k + 16, :] = running
        running = block_decay * running + got1[16 * k : 16 * k + 16, :]
    group_s[...] = running
    for d in range(7, 0, -1):
        k = group_at(*OFFSETS[d])
        copy = remote(group_s, got2.at[part(g), :], send2.at[0], recv2.at[0], seq=8 * k + i)
        copy.start()
    got2[part(g), :] = running
    landed(got2.at[seven, :], send2.at[0])
    landed(got2.at[seven, :], recv2.at[0])
    before = jnp.zeros((16, 128), F32)
    for k in range(8):
        before = jnp.where(k < g, group_decay * before + got2[16 * k : 16 * k + 16, :], before)
    for k in range(8):
        pre_s[16 * k : 16 * k + 16, :] = pre_s[16 * k : 16 * k + 16, :] + before
        before = before * block_decay
    for d in range(1, 8):
        k = lax.rem(i + d, 8)
        copy = remote(pre_s.at[part(k), :], got3.at[part(i), :], send3.at[0], recv3.at[0], seq=8 * g + k)
        copy.start()
    got3[part(i), :] = pre_s[part(i), :]
    landed(got3.at[seven, :], send3.at[0])
    landed(got3.at[seven, :], recv3.at[0])

    state = jnp.stack([got3[pl.ds(r, 8, stride=16), :] for r in range(16)], axis=0)

    def carried(block, state):
        for k in range(4):
            tile = tile_of(4 * block + k)
            state = lam * state
            full = yl_s[tile, :] + jnp.sum(state, axis=0)
            h_s[tile, :] = (mg_s[tile, :] * full).astype(BF16).astype(F32)
        return state

    lax.fori_loop(0, 32, carried, state)

    squares = jnp.zeros((128, 128), F32)
    for c in range(BLOCKS):
        block = h_s[pl.ds(c, 128, stride=8), :]
        turned = block.T
        xt_s[c] = turned.astype(BF16)
        squares = squares + turned * turned
        hy_ref[:, c * 128 : (c + 1) * 128] = block.astype(BF16)
    ss_s[ch] = jnp.sum(squares, axis=0, keepdims=True)

    for d in range(1, 4):
        k = lax.rem(ch + d, 4)
        copy = remote(ss_s.at[ch], ss_s.at[ch], sendc.at[0], recvc.at[0], ch=k)
        copy.start()
    slot = 8 * g + i
    for d in range(7, 0, -1):
        k = group_at(*OFFSETS[d])
        copy = remote(xt_s.at[k], xf_s.at[slot], senda.at[0], recva.at[d], seq=8 * k + i)
        copy.start()
    xf_s[slot] = xt_s[g]

    sources = [2 * lax.rem(y + 4 - dy, 4) + lax.rem(half + dz, 2) for dy, dz in OFFSETS]
    places = [8 * k for k in sources]
    other = 8 * g + 2 * x + 1 - core

    def along(b, to, receive):
        remote(xf_s.at[b], xf_s.at[b], sendx.at[0], receive, seq=to).start()

    def own_column(d):
        b = places[d] + i
        if d:
            landed(xf_s.at[b], recva.at[d])
        for s in range(1, 4):
            along(b, 8 * g + 2 * lax.rem(x + s, 4) + core, recvb.at[d])
        along(b, other, recvo.at[d])

    def from_x(d):
        landed(xf_s.at[pl.ds(0, 3)], recvb.at[d])
        for s in (1, 3, 2):
            along(places[d] + 2 * lax.rem(x + s, 4) + core, other, recvo.at[d])

    def row_at(i_, g_):
        return 8 * i_ + 4 * lax.rem(g_, 2) + g_ // 2

    def scales_out(z):
        rows = pl.ds(8 * i + 4 * lax.rem(half + z, 2), 4)
        landed(inv_s.at[pl.ds(0, 3 + z)], recvi.at[z])
        for d in range(1, 8):
            to = 8 * g + lax.rem(i + d, 8)
            copy = remote(inv_s.at[rows], inv_s.at[rows], sendj.at[0], recvj.at[z], seq=to)
            copy.start()

    def scales_in(z):
        landed(inv_s.at[pl.ds(0, 28)], recvj.at[z])

    query_gain = jnp.broadcast_to(qg_ref[pl.ds(g, 1), :], (128, 128)).T
    key_gain = jnp.broadcast_to(kg_ref[pl.ds(g, 1), :], (128, 128)).T

    def normed(b, i_, g_):
        return xf_s[b].astype(F32) * inv_s[row_at(i_, g_)]

    def prepare(d):
        k = sources[d]
        landed(xf_s.at[pl.ds(0, 4)], recvo.at[d])
        for n in range(8):
            rows = normed(places[d] + n, n, k)
            vt_s[k, :, 128 * n : 128 * n + 128] = rows.astype(BF16)
            kn_s[k, 128 * n : 128 * n + 128, :] = (rows * key_gain).T.astype(BF16)

    own_column(0)
    landed(ss_s.at[pl.ds(0, 3)], sendc.at[0])
    landed(ss_s.at[pl.ds(0, 3)], recvc.at[0])
    total = ss_s[0] + ss_s[1] + ss_s[2] + ss_s[3]
    inv_s[row_at(i, g)] = lax.rsqrt(total / C + EPS)
    mine = inv_s.at[row_at(i, g)]
    for d in range(7, 0, -1):
        copy = remote(mine, mine, sendi.at[0], recvi.at[d // 4], seq=8 * group_at(*OFFSETS[d]) + i)
        copy.start()
    for d in range(1, 4):
        own_column(d)
    scales_out(0)
    for d in range(4, 8):
        own_column(d)
    scales_out(1)
    for d in range(4):
        from_x(d)
    scales_in(0)
    for d in range(4):
        prepare(d)
    for n in range(8):
        q_s[:, 128 * n : 128 * n + 128] = (normed(8 * n + i, i, n) * query_gain).astype(BF16)

    factor = HEAD ** (-0.5) * math.log2(math.e)
    ahead = lax.broadcasted_iota(jnp.int32, (1024, 128), 0) - lax.broadcasted_iota(jnp.int32, (1024, 128), 1)

    def attend(n, segment, carry, masked):
        peak, total, blend = carry
        query = q_s[:, pl.ds(pl.multiple_of(128 * n, 128), 128)]
        score = jnp.dot(kn_s[segment], query, preferred_element_type=F32) * factor
        if masked:
            score = jnp.where(ahead <= 128 * i + 1024 * (n - segment), score, -1e30)
        new_peak = jnp.maximum(peak, jnp.max(score, axis=0, keepdims=True))
        weight = jnp.exp2(score - new_peak)
        shrink = jnp.exp2(peak - new_peak)
        total = total * shrink + jnp.sum(weight, axis=0, keepdims=True)
        blend = blend * shrink + jnp.dot(vt_s[segment], weight.astype(BF16), preferred_element_type=F32)
        return new_peak, total, blend

    def sweep(queries, segments, carries, chains=(3, 2, 1, 0)):
        for j in range(4):
            for m in chains:
                if m < j:
                    continue
                carries[m] = attend(2 * m + queries, 2 * j + segments, carries[m], m == j)
        return carries

    for far in (1, 0):
        carries = [
            (jnp.full((1, 128), -1e30, F32), jnp.zeros((1, 128), F32), jnp.zeros((128, 128), F32))
            for _ in range(4)
        ]
        carries = sweep(lax.rem(half + far, 2), half, carries)
        for m in range(4):
            peak_s[4 * far + m], total_s[4 * far + m], blend_s[4 * far + m] = carries[m]
        from_x(4 + 2 * (1 - far))
        from_x(5 + 2 * (1 - far))
    scales_in(1)
    for d in range(4, 8):
        prepare(d)

    columns = pl.ds(pl.multiple_of(128 * g, 128), 128)

    def given(m, far):
        n = 2 * m + lax.rem(half + far, 2)
        place = 4 * far + m
        return remote(o_s.at[place], out_ref.at[:, columns], sendr.at[0], recvr.at[0], seq=8 * n + i)

    for far, chains in ((1, (1, 0)), (1, (3, 2)), (0, (3, 2, 1, 0))):
        carries = {m: (peak_s[4 * far + m], total_s[4 * far + m], blend_s[4 * far + m]) for m in chains}
        carries = sweep(lax.rem(half + far, 2), 1 - half, carries, chains)
        for m in chains:
            o_s[4 * far + m] = (carries[m][2] / carries[m][1]).T.astype(BF16)
        for m in chains:
            if far:
                given(m, far).start()
            else:
                pl.when(y != m)(given(m, far).start)
    out_ref[:, columns] = o_s[y]
    landed(o_s.at[pl.ds(0, 7)], recvr.at[0])
    landed(o_s.at[pl.ds(0, 7)], sendr.at[0])
    landed(xf_s.at[pl.ds(0, 7)], senda.at[0])
    landed(xf_s.at[pl.ds(0, 56)], sendx.at[0])
    landed(inv_s.at[pl.ds(0, 7)], sendi.at[0])
    landed(inv_s.at[pl.ds(0, 56)], sendj.at[0])


def finish_kernel(hy_in, out_in, hy_ref, out_ref, semaphores):
    copies = [
        pltpu.make_async_copy(hy_in, hy_ref, semaphores.at[0]),
        pltpu.make_async_copy(out_in, out_ref, semaphores.at[1]),
    ]
    for copy in copies:
        copy.start()
    for copy in copies:
        copy.wait()


def vmem(*shape, dtype=F32):
    return pltpu.VMEM(shape, dtype)


def in_vmem(count):
    return [pl.BlockSpec(memory_space=pltpu.VMEM)] * count


def dmas(count):
    return pltpu.SemaphoreType.DMA((count,))


def on_device(
    token_ids, embedding, short_filter, medium_filter, long_residue, long_rate, query_gain, key_gain
):
    shape = jax.ShapeDtypeStruct
    counts = (2, 2, 1, 1, 1, 1, 1, 1, 1, 1, 1, 2, 1, 2, 1, 1, 8, 8, 8, 1, 1)
    results = pl.pallas_call(
        whole_kernel,
        out_shape=[shape((TOK, 1024), BF16), shape((TOK, 1024), BF16)],
        in_specs=in_vmem(1) + [pl.BlockSpec(memory_space=pl.ANY)] * 5 + in_vmem(2),
        out_specs=in_vmem(2),
        scratch_shapes=[
            vmem(512, 1024, dtype=BF16), vmem(7, 1024), vmem(128, 1024), vmem(16, 1024), vmem(16, 1024), dmas(5),
            vmem(1, 128, dtype=jnp.int32), vmem(1, 128, dtype=jnp.int32),
            vmem(2176, 128), vmem(2048, 128), vmem(64, 128), vmem(1024, 128), vmem(128, 128), vmem(128, 128),
            vmem(1024, 128), vmem(1024, 128), vmem(128, 128),
            vmem(128, 128), vmem(128, 128), vmem(128, 128), vmem(128, 128), vmem(16, 128),
            vmem(1024, 128), vmem(8, 128, 128, dtype=BF16), vmem(4, 1, 128), vmem(64, 1, 128),
            vmem(64, 128, 128, dtype=BF16), vmem(8, 1024, 128, dtype=BF16), vmem(8, 128, 1024, dtype=BF16),
            vmem(128, 1024, dtype=BF16), vmem(8, 128, 128, dtype=BF16),
            vmem(8, 1, 128), vmem(8, 1, 128), vmem(8, 128, 128),
        ]
        + [dmas(count) for count in counts],
        compiler_params=pltpu.CompilerParams(vmem_limit_bytes=LIMIT, collective_id=0, has_side_effects=True),
        name="whole",
    )(
        token_ids.reshape(1, TOK), embedding, short_filter, medium_filter, long_residue, long_rate,
        query_gain.reshape(8, 128), key_gain.reshape(8, 128),
    )
    return pl.pallas_call(
        finish_kernel,
        out_shape=[shape((TOK, 1024), BF16), shape((TOK, 1024), BF16)],
        in_specs=[pl.BlockSpec(memory_space=pl.ANY)] * 2,
        out_specs=in_vmem(2),
        scratch_shapes=[dmas(2)],
        name="finish",
    )(*results)


def solution(mesh):
    in_specs = (
        P("seq"),
        P(None, "ch"),
        P(None, "ch"),
        P(None, "ch"),
        P(None, "ch"),
        P(None, "ch"),
        P("ch"),
        P("ch"),
    )
    out_specs = (P("seq", "ch"), P("seq", "ch"))
    return jax.shard_map(
        on_device, mesh=mesh, in_specs=in_specs, out_specs=out_specs, check_vma=False
    )
```

```python
import math

import jax
import jax.numpy as jnp
from jax import lax
from jax.experimental import pallas as pl
from jax.experimental.pallas import tpu as pltpu
from jax.sharding import PartitionSpec as P

C = 4096
HEAD = 128
EPS = 1e-05
TOK = 128
BLOCKS = 8
MESH = pl.DeviceIdType.MESH
F32 = jnp.float32
BF16 = jnp.bfloat16
LIMIT = 60 << 20

OFFSETS = ((0, 0), (1, 0), (3, 0), (2, 0), (0, 1), (1, 1), (3, 1), (2, 1))


def rows_of(step):
    return pl.ds(pl.multiple_of(8 * step, 8), 128)


def part(k):
    return pl.ds(pl.multiple_of(16 * k, 16), 16)


def here():
    seq = lax.axis_index("seq")
    return seq, seq // 8, lax.rem(seq, 8)


def remote(source, target, send, receive, **where):
    return pltpu.make_async_remote_copy(
        src_ref=source, dst_ref=target, send_sem=send, recv_sem=receive, device_id=where, device_id_type=MESH
    )


def landed(ref, semaphore):
    pltpu.make_async_copy(ref, ref, semaphore).wait()


def embed(tokens, emb_ref, e_s, first, keep):
    column = jnp.broadcast_to(tokens.astype(F32), (128, 128)).T[128 - keep :]
    lane = lax.broadcasted_iota(jnp.int32, column.shape, 1).astype(F32)
    one_hot = jnp.concatenate(
        [jnp.where(column == lane + 128.0 * k, 1.0, 0.0).astype(BF16) for k in range(4)], axis=1
    )
    for pair in range(4):
        rows = jnp.dot(one_hot, emb_ref[:, pair * 256 : pair * 256 + 256], preferred_element_type=F32)
        for k in range(2):
            e_s[pl.ds(8 * first + 2 * pair + k, keep, stride=8), :] = rows[:, k * 128 : k * 128 + 128]


def whole_kernel(
    tok_in, emb_in, short_in, med_in, res_in, rate_in, qg_in, kg_in, hy_ref, out_ref,
    tok_ref, emb_ref, short_ref, med_ref, res_ref, rate_ref, qg_ref, kg_ref, fetch,
    near_s, far_s, e_s, sg_s, sw_s, mw_s, cf_s, lam_s, mg_s, yl_s, end_s,
    got1, got2, got3, pre_s, group_s, h_s, xt_s, ss_s, inv_s, xf_s, kn_s, vt_s, q_s, o_s,
    peak_s, total_s, blend_s,
    sendt, recvt, send1, recv1, send2, recv2, send3, recv3, sendc, recvc, sendi, recvi, sendj, recvj,
    senda, sendx, recva, recvb, recvo, sendr, recvr,
):
    seq, g, i = here()
    ch = lax.axis_index("ch")
    y, half, x, core = g // 2, lax.rem(g, 2), i // 2, lax.rem(i, 2)

    def group_at(dy, dz):
        return 2 * lax.rem(y + dy, 4) + lax.rem(half + dz, 2)

    names = [{"seq": 8 * g + lax.rem(i + d, 8)} for d in range(1, 8)]
    names += [{"seq": 8 * lax.rem(g + d, 8) + i} for d in range(1, 8)]
    names += [{"ch": lax.rem(ch + d, 4)} for d in range(1, 4)]
    names += [{"seq": lax.rem(seq + d, 64)} for d in (1, 2, 62, 63)]
    barrier = pltpu.get_barrier_semaphore()
    for where in names:
        pl.semaphore_signal(barrier, inc=1, device_id=where, device_id_type=MESH)

    fetches = [
        pltpu.make_async_copy(source, target, fetch.at[n])
        for n, (source, target) in enumerate(
            [
                (tok_in, tok_ref), (rate_in, rate_ref), (res_in, res_ref), (short_in, short_ref),
                (med_in, med_ref), (emb_in, emb_ref), (qg_in, qg_ref), (kg_in, kg_ref),
            ]
        )
    ]
    for copy in fetches:
        copy.start()
    fetches[0].wait()
    pl.semaphore_wait(barrier, len(names))
    tokens = [
        remote(tok_ref, near_s, sendt.at[0], recvt.at[0], seq=lax.rem(seq + 1, 64)),
        remote(tok_ref, far_s, sendt.at[1], recvt.at[1], seq=lax.rem(seq + 2, 64)),
    ]
    for copy in tokens:
        copy.start()
    for copy in fetches[1:]:
        copy.wait()

    for c in range(BLOCKS):
        lanes = slice(c * 128, (c + 1) * 128)
        sw_s[pl.ds(c, 7, stride=8), :] = short_ref[:, lanes]
        mw_s[pl.ds(c, 128, stride=8), :] = med_ref[:, lanes]
        lam_s[pl.ds(c, 16, stride=8), :] = rate_ref[:, lanes]
        cf_s[pl.ds(c, 16, stride=8), :] = res_ref[:, lanes]
    rate = lam_s[...]
    twice = 2.0 * rate
    tail = jnp.ones_like(twice)
    for k in range(9, 1, -1):
        tail = 1.0 - twice * (1.0 / k) * tail
    cf_s[...] = cf_s[...] * jnp.sqrt(twice * tail) * 0.25
    lam_s[...] = jnp.exp(-rate)
    embed(tok_ref[...], emb_ref, e_s, 144, 128)

    def short_block(block, _):
        first = 16 + block * 16
        own = e_s[rows_of(first), :].reshape(16, 8, 128)
        total = own * sw_s[0:8, :]
        for j in range(1, 7):
            total = total + e_s[rows_of(first - j), :].reshape(16, 8, 128) * sw_s[8 * j : 8 * j + 8, :]
        gated = (own * total).astype(BF16).astype(F32)
        sg_s[rows_of(16 * block), :] = gated.reshape(128, 128)
        return 0

    lax.fori_loop(9, 16, short_block, 0)

    def taps_of(block):
        def taps(chunk, total):
            base = 128 + 16 * block - 16 * chunk - 15
            window = sg_s[pl.ds(pl.multiple_of(8 * base, 8), 31 * 8), :].reshape(31, 8, 128)
            weight = mw_s[rows_of(16 * chunk), :].reshape(16, 8, 128)
            for j in range(16):
                total = total + weight[j][None] * window[15 - j : 31 - j]
            return total

        return taps

    def medium_start(block, _):
        total = lax.fori_loop(0, block - 1, taps_of(block), jnp.zeros((16, 8, 128), F32))
        mg_s[rows_of(16 * block), :] = total.reshape(128, 128)
        return 0

    mg_s[0:256, :] = jnp.zeros((256, 128), F32)
    lax.fori_loop(2, 8, medium_start, 0)
    for copy in tokens:
        copy.wait()
    embed(jnp.where(seq >= 1, near_s[...], -1), emb_ref, e_s, 16, 128)
    embed(jnp.where(seq >= 2, far_s[...], -1), emb_ref, e_s, 0, 16)
    lax.fori_loop(0, 9, short_block, 0)

    def medium_block(block, _):
        total = mg_s[rows_of(16 * block), :].reshape(16, 8, 128)
        total = lax.fori_loop(jnp.maximum(block - 1, 0), 8, taps_of(block), total)
        own = sg_s[rows_of(128 + 16 * block), :].reshape(16, 8, 128)
        gated = (own * total).astype(BF16).astype(F32)
        mg_s[rows_of(16 * block), :] = gated.reshape(128, 128)
        return 0

    lax.fori_loop(0, 8, medium_block, 0)

    lam = lam_s[...].reshape(16, 8, 128)
    coef = cf_s[...].reshape(16, 8, 128)

    def tile_of(step):
        return pl.ds(pl.multiple_of(8 * step, 8), 8)

    def forget(block, state):
        for k in range(8):
            state = lam * state + coef * mg_s[tile_of(8 * block + k), :][None]
        return state

    state = lax.fori_loop(0, 16, forget, jnp.zeros((16, 8, 128), F32))
    for r in range(16):
        end_s[pl.ds(r, 8, stride=16), :] = state[r]

    seven = pl.ds(0, 112)
    for d in range(1, 8):
        k = lax.rem(i + d, 8)
        copy = remote(end_s.at[part(k), :], got1.at[part(i), :], send1.at[0], recv1.at[0], seq=8 * g + k)
        copy.start()
    got1[part(i), :] = end_s[part(i), :]

    def local(block, state):
        for k in range(4):
            tile = tile_of(4 * block + k)
            state = lam * state + coef * mg_s[tile, :][None]
            yl_s[tile, :] = jnp.sum(state, axis=0)
        return state

    lax.fori_loop(0, 32, local, jnp.zeros((16, 8, 128), F32))
    rate = rate_ref[:, pl.ds(pl.multiple_of(128 * i, 128), 128)]
    block_decay = jnp.exp(-128.0 * rate)
    group_decay = jnp.exp(-1024.0 * rate)
    landed(got1.at[seven, :], send1.at[0])
    landed(got1.at[seven, :], recv1.at[0])
    running = jnp.zeros((16, 128), F32)
    for k in range(8):
        pre_s[16 * k : 16 * k + 16, :] = running
        running = block_decay * running + got1[16 * k : 16 * k + 16, :]
    group_s[...] = running
    for d in range(7, 0, -1):
        k = group_at(*OFFSETS[d])
        copy = remote(group_s, got2.at[part(g), :], send2.at[0], recv2.at[0], seq=8 * k + i)
        copy.start()
    got2[part(g), :] = running
    landed(got2.at[seven, :], send2.at[0])
    landed(got2.at[seven, :], recv2.at[0])
    before = jnp.zeros((16, 128), F32)
    for k in range(8):
        before = jnp.where(k < g, group_decay * before + got2[16 * k : 16 * k + 16, :], before)
    for k in range(8):
        pre_s[16 * k : 16 * k + 16, :] = pre_s[16 * k : 16 * k + 16, :] + before
        before = before * block_decay
    for d in range(1, 8):
        k = lax.rem(i + d, 8)
        copy = remote(pre_s.at[part(k), :], got3.at[part(i), :], send3.at[0], recv3.at[0], seq=8 * g + k)
        copy.start()
    got3[part(i), :] = pre_s[part(i), :]
    landed(got3.at[seven, :], send3.at[0])
    landed(got3.at[seven, :], recv3.at[0])

    state = jnp.stack([got3[pl.ds(r, 8, stride=16), :] for r in range(16)], axis=0)

    def carried(block, state):
        for k in range(4):
            tile = tile_of(4 * block + k)
            state = lam * state
            full = yl_s[tile, :] + jnp.sum(state, axis=0)
            h_s[tile, :] = (mg_s[tile, :] * full).astype(BF16).astype(F32)
        return state

    lax.fori_loop(0, 32, carried, state)

    squares = jnp.zeros((128, 128), F32)
    for c in range(BLOCKS):
        block = h_s[pl.ds(c, 128, stride=8), :]
        turned = block.T
        xt_s[c] = turned.astype(BF16)
        squares = squares + turned * turned
        hy_ref[:, c * 128 : (c + 1) * 128] = block.astype(BF16)
    ss_s[ch] = jnp.sum(squares, axis=0, keepdims=True)

    for d in range(1, 4):
        k = lax.rem(ch + d, 4)
        copy = remote(ss_s.at[ch], ss_s.at[ch], sendc.at[0], recvc.at[0], ch=k)
        copy.start()
    slot = 8 * g + i
    for d in range(7, 0, -1):
        k = group_at(*OFFSETS[d])
        copy = remote(xt_s.at[k], xf_s.at[slot], senda.at[0], recva.at[d], seq=8 * k + i)
        copy.start()
    xf_s[slot] = xt_s[g]

    sources = [2 * lax.rem(y + 4 - dy, 4) + lax.rem(half + dz, 2) for dy, dz in OFFSETS]
    places = [8 * k for k in sources]
    other = 8 * g + 2 * x + 1 - core

    def along(b, to, receive):
        remote(xf_s.at[b], xf_s.at[b], sendx.at[0], receive, seq=to).start()

    def own_column(d):
        b = places[d] + i
        if d:
            landed(xf_s.at[b], recva.at[d])
        for s in range(1, 4):
            along(b, 8 * g + 2 * lax.rem(x + s, 4) + core, recvb.at[d])
        along(b, other, recvo.at[d])

    def from_x(d):
        landed(xf_s.at[pl.ds(0, 3)], recvb.at[d])
        for s in (1, 3, 2):
            along(places[d] + 2 * lax.rem(x + s, 4) + core, other, recvo.at[d])

    def row_at(i_, g_):
        return 8 * i_ + 4 * lax.rem(g_, 2) + g_ // 2

    def scales_out(z):
        rows = pl.ds(8 * i + 4 * lax.rem(half + z, 2), 4)
        landed(inv_s.at[pl.ds(0, 3 + z)], recvi.at[z])
        for d in range(1, 8):
            to = 8 * g + lax.rem(i + d, 8)
            copy = remote(inv_s.at[rows], inv_s.at[rows], sendj.at[0], recvj.at[z], seq=to)
            copy.start()

    def scales_in(z):
        landed(inv_s.at[pl.ds(0, 28)], recvj.at[z])

    query_gain = jnp.broadcast_to(qg_ref[pl.ds(g, 1), :], (128, 128)).T
    key_gain = jnp.broadcast_to(kg_ref[pl.ds(g, 1), :], (128, 128)).T

    def normed(b, i_, g_):
        return xf_s[b].astype(F32) * inv_s[row_at(i_, g_)]

    def prepare(d):
        k = sources[d]
        landed(xf_s.at[pl.ds(0, 4)], recvo.at[d])
        for n in range(8):
            rows = normed(places[d] + n, n, k)
            vt_s[k, :, 128 * n : 128 * n + 128] = rows.astype(BF16)
            kn_s[k, 128 * n : 128 * n + 128, :] = (rows * key_gain).T.astype(BF16)

    own_column(0)
    landed(ss_s.at[pl.ds(0, 3)], sendc.at[0])
    landed(ss_s.at[pl.ds(0, 3)], recvc.at[0])
    total = ss_s[0] + ss_s[1] + ss_s[2] + ss_s[3]
    inv_s[row_at(i, g)] = lax.rsqrt(total / C + EPS)
    mine = inv_s.at[row_at(i, g)]
    for d in range(7, 0, -1):
        copy = remote(mine, mine, sendi.at[0], recvi.at[d // 4], seq=8 * group_at(*OFFSETS[d]) + i)
        copy.start()
    for d in range(1, 4):
        own_column(d)
    scales_out(0)
    for d in range(4, 8):
        own_column(d)
    scales_out(1)
    for d in range(4):
        from_x(d)
    scales_in(0)
    for d in range(4):
        prepare(d)
    for n in range(8):
        q_s[:, 128 * n : 128 * n + 128] = (normed(8 * n + i, i, n) * query_gain).astype(BF16)

    factor = HEAD ** (-0.5) * math.log2(math.e)
    ahead = lax.broadcasted_iota(jnp.int32, (1024, 128), 0) - lax.broadcasted_iota(jnp.int32, (1024, 128), 1)

    def attend(n, segment, carry, masked):
        peak, total, blend = carry
        query = q_s[:, pl.ds(pl.multiple_of(128 * n, 128), 128)]
        score = jnp.dot(kn_s[segment], query, preferred_element_type=F32) * factor
        if masked:
            score = jnp.where(ahead <= 128 * i + 1024 * (n - segment), score, -1e30)
        new_peak = jnp.maximum(peak, jnp.max(score, axis=0, keepdims=True))
        weight = jnp.exp2(score - new_peak)
        shrink = jnp.exp2(peak - new_peak)
        total = total * shrink + jnp.sum(weight, axis=0, keepdims=True)
        blend = blend * shrink + jnp.dot(vt_s[segment], weight.astype(BF16), preferred_element_type=F32)
        return new_peak, total, blend

    def sweep(queries, segments, carries, chains=(3, 2, 1, 0)):
        for j in range(4):
            for m in chains:
                if m < j:
                    continue
                carries[m] = attend(2 * m + queries, 2 * j + segments, carries[m], m == j)
        return carries

    for far in (1, 0):
        carries = [
            (jnp.full((1, 128), -1e30, F32), jnp.zeros((1, 128), F32), jnp.zeros((128, 128), F32))
            for _ in range(4)
        ]
        carries = sweep(lax.rem(half + far, 2), half, carries)
        for m in range(4):
            peak_s[4 * far + m], total_s[4 * far + m], blend_s[4 * far + m] = carries[m]
        from_x(4 + 2 * (1 - far))
        from_x(5 + 2 * (1 - far))
    scales_in(1)
    for d in range(4, 8):
        prepare(d)

    columns = pl.ds(pl.multiple_of(128 * g, 128), 128)

    def given(m, far):
        n = 2 * m + lax.rem(half + far, 2)
        place = 4 * far + m
        return remote(o_s.at[place], out_ref.at[:, columns], sendr.at[0], recvr.at[0], seq=8 * n + i)

    for far, chains in ((1, (1, 0)), (1, (3, 2)), (0, (3, 2, 1, 0))):
        carries = {m: (peak_s[4 * far + m], total_s[4 * far + m], blend_s[4 * far + m]) for m in chains}
        carries = sweep(lax.rem(half + far, 2), 1 - half, carries, chains)
        for m in chains:
            o_s[4 * far + m] = (carries[m][2] / carries[m][1]).T.astype(BF16)
        for m in chains:
            if far:
                given(m, far).start()
            else:
                pl.when(y != m)(given(m, far).start)
    out_ref[:, columns] = o_s[y]
    landed(o_s.at[pl.ds(0, 7)], recvr.at[0])
    landed(o_s.at[pl.ds(0, 7)], sendr.at[0])
    landed(xf_s.at[pl.ds(0, 7)], senda.at[0])
    landed(xf_s.at[pl.ds(0, 56)], sendx.at[0])
    landed(inv_s.at[pl.ds(0, 7)], sendi.at[0])
    landed(inv_s.at[pl.ds(0, 56)], sendj.at[0])


def finish_kernel(hy_in, out_in, hy_ref, out_ref, semaphores):
    copies = [
        pltpu.make_async_copy(hy_in, hy_ref, semaphores.at[0]),
        pltpu.make_async_copy(out_in, out_ref, semaphores.at[1]),
    ]
    for copy in copies:
        copy.start()
    for copy in copies:
        copy.wait()


def vmem(*shape, dtype=F32):
    return pltpu.VMEM(shape, dtype)


def in_vmem(count):
    return [pl.BlockSpec(memory_space=pltpu.VMEM)] * count


def dmas(count):
    return pltpu.SemaphoreType.DMA((count,))


def on_device(
    token_ids, embedding, short_filter, medium_filter, long_residue, long_rate, query_gain, key_gain
):
    shape = jax.ShapeDtypeStruct
    counts = (2, 2, 1, 1, 1, 1, 1, 1, 1, 1, 1, 2, 1, 2, 1, 1, 8, 8, 8, 1, 1)
    results = pl.pallas_call(
        whole_kernel,
        out_shape=[shape((TOK, 1024), BF16), shape((TOK, 1024), BF16)],
        in_specs=[pl.BlockSpec(memory_space=pl.ANY)] * 8,
        out_specs=in_vmem(2),
        scratch_shapes=[
            vmem(1, 128, dtype=jnp.int32), vmem(512, 1024, dtype=BF16), vmem(7, 1024), vmem(128, 1024),
            vmem(16, 1024), vmem(16, 1024), vmem(8, 128), vmem(8, 128), dmas(8),
            vmem(1, 128, dtype=jnp.int32), vmem(1, 128, dtype=jnp.int32),
            vmem(2176, 128), vmem(2048, 128), vmem(64, 128), vmem(1024, 128), vmem(128, 128), vmem(128, 128),
            vmem(1024, 128), vmem(1024, 128), vmem(128, 128),
            vmem(128, 128), vmem(128, 128), vmem(128, 128), vmem(128, 128), vmem(16, 128),
            vmem(1024, 128), vmem(8, 128, 128, dtype=BF16), vmem(4, 1, 128), vmem(64, 1, 128),
            vmem(64, 128, 128, dtype=BF16), vmem(8, 1024, 128, dtype=BF16), vmem(8, 128, 1024, dtype=BF16),
            vmem(128, 1024, dtype=BF16), vmem(8, 128, 128, dtype=BF16),
            vmem(8, 1, 128), vmem(8, 1, 128), vmem(8, 128, 128),
        ]
        + [dmas(count) for count in counts],
        compiler_params=pltpu.CompilerParams(vmem_limit_bytes=LIMIT, collective_id=0, has_side_effects=True),
        name="whole",
    )(
        token_ids.reshape(1, TOK), embedding, short_filter, medium_filter, long_residue, long_rate,
        query_gain.reshape(8, 128), key_gain.reshape(8, 128),
    )
    return pl.pallas_call(
        finish_kernel,
        out_shape=[shape((TOK, 1024), BF16), shape((TOK, 1024), BF16)],
        in_specs=[pl.BlockSpec(memory_space=pl.ANY)] * 2,
        out_specs=in_vmem(2),
        scratch_shapes=[dmas(2)],
        name="finish",
    )(*results)


def solution(mesh):
    in_specs = (
        P("seq"),
        P(None, "ch"),
        P(None, "ch"),
        P(None, "ch"),
        P(None, "ch"),
        P(None, "ch"),
        P("ch"),
        P("ch"),
    )
    out_specs = (P("seq", "ch"), P("seq", "ch"))
    return jax.shard_map(
        on_device, mesh=mesh, in_specs=in_specs, out_specs=out_specs, check_vma=False
    )
```

```python
import math

import jax
import jax.numpy as jnp
from jax import lax
from jax.experimental import pallas as pl
from jax.experimental.pallas import tpu as pltpu
from jax.sharding import PartitionSpec as P

C = 4096
HEAD = 128
EPS = 1e-05
TOK = 128
BLOCKS = 8
MESH = pl.DeviceIdType.MESH
F32 = jnp.float32
BF16 = jnp.bfloat16
LIMIT = 60 << 20

OFFSETS = ((0, 0), (1, 0), (3, 0), (2, 0), (0, 1), (1, 1), (3, 1), (2, 1))


def rows_of(step):
    return pl.ds(pl.multiple_of(8 * step, 8), 128)


def part(k):
    return pl.ds(pl.multiple_of(16 * k, 16), 16)


def here():
    seq = lax.axis_index("seq")
    return seq, seq // 8, lax.rem(seq, 8)


def remote(source, target, send, receive, **where):
    return pltpu.make_async_remote_copy(
        src_ref=source, dst_ref=target, send_sem=send, recv_sem=receive, device_id=where, device_id_type=MESH
    )


def landed(ref, semaphore):
    pltpu.make_async_copy(ref, ref, semaphore).wait()


def embed(tokens, emb_ref, e_s, first, keep):
    column = jnp.broadcast_to(tokens.astype(F32), (128, 128)).T[128 - keep :]
    lane = lax.broadcasted_iota(jnp.int32, column.shape, 1).astype(F32)
    one_hot = jnp.concatenate(
        [jnp.where(column == lane + 128.0 * k, 1.0, 0.0).astype(BF16) for k in range(4)], axis=1
    )
    for pair in range(4):
        rows = jnp.dot(one_hot, emb_ref[:, pair * 256 : pair * 256 + 256], preferred_element_type=F32)
        for k in range(2):
            e_s[pl.ds(8 * first + 2 * pair + k, keep, stride=8), :] = rows[:, k * 128 : k * 128 + 128]


def whole_kernel(
    tok_in, emb_in, short_in, med_in, res_in, rate_in, qg_in, kg_in, hy_ref, out_ref,
    tok_ref, emb_ref, short_ref, med_ref, res_ref, rate_ref, qg_ref, kg_ref, fetch,
    near_s, far_s, e_s, sg_s, sw_s, mw_s, cf_s, lam_s, mg_s, yl_s, end_s,
    got1, got2, got3, pre_s, group_s, h_s, xt_s, ss_s, inv_s, xf_s, kn_s, vt_s, q_s, o_s,
    peak_s, total_s, blend_s,
    sendt, recvt, send1, recv1, send2, recv2, send3, recv3, sendc, recvc, sendi, recvi, sendj, recvj,
    senda, sendx, recva, recvb, recvo, sendr, recvr,
):
    seq, g, i = here()
    ch = lax.axis_index("ch")
    y, half, x, core = g // 2, lax.rem(g, 2), i // 2, lax.rem(i, 2)

    def group_at(dy, dz):
        return 2 * lax.rem(y + dy, 4) + lax.rem(half + dz, 2)

    names = [{"seq": 8 * g + lax.rem(i + d, 8)} for d in range(1, 8)]
    names += [{"seq": 8 * lax.rem(g + d, 8) + i} for d in range(1, 8)]
    names += [{"ch": lax.rem(ch + d, 4)} for d in range(1, 4)]
    names += [{"seq": lax.rem(seq + d, 64)} for d in (1, 2, 62, 63)]
    barrier = pltpu.get_barrier_semaphore()
    for where in names:
        pl.semaphore_signal(barrier, inc=1, device_id=where, device_id_type=MESH)

    fetches = [
        pltpu.make_async_copy(source, target, fetch.at[n])
        for n, (source, target) in enumerate(
            [
                (tok_in, tok_ref), (rate_in, rate_ref), (res_in, res_ref), (short_in, short_ref),
                (med_in, med_ref), (emb_in, emb_ref), (qg_in, qg_ref), (kg_in, kg_ref),
            ]
        )
    ]
    for copy in fetches:
        copy.start()
    fetches[0].wait()
    pl.semaphore_wait(barrier, len(names))
    tokens = [
        remote(tok_ref, near_s, sendt.at[0], recvt.at[0], seq=lax.rem(seq + 1, 64)),
        remote(tok_ref, far_s, sendt.at[1], recvt.at[1], seq=lax.rem(seq + 2, 64)),
    ]
    for copy in tokens:
        copy.start()
    for copy in fetches[1:]:
        copy.wait()

    for c in range(BLOCKS):
        lanes = slice(c * 128, (c + 1) * 128)
        sw_s[pl.ds(c, 7, stride=8), :] = short_ref[:, lanes]
        mw_s[pl.ds(c, 128, stride=8), :] = med_ref[:, lanes]
        lam_s[pl.ds(c, 16, stride=8), :] = rate_ref[:, lanes]
        cf_s[pl.ds(c, 16, stride=8), :] = res_ref[:, lanes]
    rate = lam_s[...]
    twice = 2.0 * rate
    tail = jnp.ones_like(twice)
    for k in range(9, 1, -1):
        tail = 1.0 - twice * (1.0 / k) * tail
    cf_s[...] = cf_s[...] * jnp.sqrt(twice * tail) * 0.25
    lam_s[...] = jnp.exp(-rate)
    embed(tok_ref[...], emb_ref, e_s, 144, 128)

    def short_block(block, _):
        first = 16 + block * 16
        own = e_s[rows_of(first), :].reshape(16, 8, 128)
        total = own * sw_s[0:8, :]
        for j in range(1, 7):
            total = total + e_s[rows_of(first - j), :].reshape(16, 8, 128) * sw_s[8 * j : 8 * j + 8, :]
        gated = (own * total).astype(BF16).astype(F32)
        sg_s[rows_of(16 * block), :] = gated.reshape(128, 128)
        return 0

    lax.fori_loop(9, 16, short_block, 0)

    def taps_of(block):
        def taps(chunk, total):
            base = 128 + 16 * block - 16 * chunk - 15
            window = sg_s[pl.ds(pl.multiple_of(8 * base, 8), 31 * 8), :].reshape(31, 8, 128)
            weight = mw_s[rows_of(16 * chunk), :].reshape(16, 8, 128)
            for j in range(16):
                total = total + weight[j][None] * window[15 - j : 31 - j]
            return total

        return taps

    def medium_start(block, _):
        total = lax.fori_loop(0, block - 1, taps_of(block), jnp.zeros((16, 8, 128), F32))
        mg_s[rows_of(16 * block), :] = total.reshape(128, 128)
        return 0

    mg_s[0:256, :] = jnp.zeros((256, 128), F32)
    lax.fori_loop(2, 8, medium_start, 0)
    for copy in tokens:
        copy.wait()
    embed(jnp.where(seq >= 1, near_s[...], -1), emb_ref, e_s, 16, 128)
    embed(jnp.where(seq >= 2, far_s[...], -1), emb_ref, e_s, 0, 16)
    lax.fori_loop(0, 9, short_block, 0)

    def medium_block(block, _):
        total = mg_s[rows_of(16 * block), :].reshape(16, 8, 128)
        total = lax.fori_loop(jnp.maximum(block - 1, 0), 8, taps_of(block), total)
        own = sg_s[rows_of(128 + 16 * block), :].reshape(16, 8, 128)
        gated = (own * total).astype(BF16).astype(F32)
        mg_s[rows_of(16 * block), :] = gated.reshape(128, 128)
        return 0

    lax.fori_loop(0, 8, medium_block, 0)

    lam = lam_s[...].reshape(16, 8, 128)
    coef = cf_s[...].reshape(16, 8, 128)

    def tile_of(step):
        return pl.ds(pl.multiple_of(8 * step, 8), 8)

    def forget(block, state):
        for k in range(8):
            state = lam * state + coef * mg_s[tile_of(8 * block + k), :][None]
        return state

    state = lax.fori_loop(0, 16, forget, jnp.zeros((16, 8, 128), F32))
    for r in range(16):
        end_s[pl.ds(r, 8, stride=16), :] = state[r]

    seven = pl.ds(0, 112)
    for d in range(1, 8):
        k = lax.rem(i + d, 8)
        copy = remote(end_s.at[part(k), :], got1.at[part(i), :], send1.at[0], recv1.at[0], seq=8 * g + k)
        copy.start()
    got1[part(i), :] = end_s[part(i), :]

    def local(block, state):
        for k in range(4):
            tile = tile_of(4 * block + k)
            state = lam * state + coef * mg_s[tile, :][None]
            yl_s[tile, :] = jnp.sum(state, axis=0)
        return state

    lax.fori_loop(0, 32, local, jnp.zeros((16, 8, 128), F32))
    rate = rate_ref[:, pl.ds(pl.multiple_of(128 * i, 128), 128)]
    block_decay = jnp.exp(-128.0 * rate)
    group_decay = jnp.exp(-1024.0 * rate)
    landed(got1.at[seven, :], send1.at[0])
    landed(got1.at[seven, :], recv1.at[0])
    running = jnp.zeros((16, 128), F32)
    for k in range(8):
        pre_s[16 * k : 16 * k + 16, :] = running
        running = block_decay * running + got1[16 * k : 16 * k + 16, :]
    group_s[...] = running
    for d in range(7, 0, -1):
        k = group_at(*OFFSETS[d])
        copy = remote(group_s, got2.at[part(g), :], send2.at[0], recv2.at[0], seq=8 * k + i)
        copy.start()
    got2[part(g), :] = running
    landed(got2.at[seven, :], send2.at[0])
    landed(got2.at[seven, :], recv2.at[0])
    before = jnp.zeros((16, 128), F32)
    for k in range(8):
        before = jnp.where(k < g, group_decay * before + got2[16 * k : 16 * k + 16, :], before)
    for k in range(8):
        pre_s[16 * k : 16 * k + 16, :] = pre_s[16 * k : 16 * k + 16, :] + before
        before = before * block_decay
    for d in range(1, 8):
        k = lax.rem(i + d, 8)
        copy = remote(pre_s.at[part(k), :], got3.at[part(i), :], send3.at[0], recv3.at[0], seq=8 * g + k)
        copy.start()
    got3[part(i), :] = pre_s[part(i), :]
    landed(got3.at[seven, :], send3.at[0])
    landed(got3.at[seven, :], recv3.at[0])

    state = jnp.stack([got3[pl.ds(r, 8, stride=16), :] for r in range(16)], axis=0)

    def carried(block, state):
        for k in range(4):
            tile = tile_of(4 * block + k)
            state = lam * state
            full = yl_s[tile, :] + jnp.sum(state, axis=0)
            h_s[tile, :] = (mg_s[tile, :] * full).astype(BF16).astype(F32)
        return state

    lax.fori_loop(0, 32, carried, state)

    squares = jnp.zeros((128, 128), F32)
    for c in range(BLOCKS):
        block = h_s[pl.ds(c, 128, stride=8), :]
        turned = block.T
        xt_s[c] = turned.astype(BF16)
        squares = squares + turned * turned
        hy_ref[:, c * 128 : (c + 1) * 128] = block.astype(BF16)
    ss_s[ch] = jnp.sum(squares, axis=0, keepdims=True)

    for d in range(1, 4):
        k = lax.rem(ch + d, 4)
        copy = remote(ss_s.at[ch], ss_s.at[ch], sendc.at[0], recvc.at[0], ch=k)
        copy.start()
    slot = 8 * g + i
    for d in range(7, 0, -1):
        k = group_at(*OFFSETS[d])
        copy = remote(xt_s.at[k], xf_s.at[slot], senda.at[0], recva.at[d], seq=8 * k + i)
        copy.start()
    xf_s[slot] = xt_s[g]

    sources = [2 * lax.rem(y + 4 - dy, 4) + lax.rem(half + dz, 2) for dy, dz in OFFSETS]
    places = [8 * k for k in sources]
    other = 8 * g + 2 * x + 1 - core

    def along(b, to, receive):
        remote(xf_s.at[b], xf_s.at[b], sendx.at[0], receive, seq=to).start()

    def own_column(d):
        b = places[d] + i
        if d:
            landed(xf_s.at[b], recva.at[d])
        for s in range(1, 4):
            along(b, 8 * g + 2 * lax.rem(x + s, 4) + core, recvb.at[d])
        along(b, other, recvo.at[d])

    def from_x(d):
        landed(xf_s.at[pl.ds(0, 3)], recvb.at[d])
        for s in (1, 3, 2):
            along(places[d] + 2 * lax.rem(x + s, 4) + core, other, recvo.at[d])

    def row_at(i_, g_):
        return 8 * i_ + 4 * lax.rem(g_, 2) + g_ // 2

    def scales_out(z):
        rows = pl.ds(8 * i + 4 * lax.rem(half + z, 2), 4)
        landed(inv_s.at[pl.ds(0, 3 + z)], recvi.at[z])
        for d in range(1, 8):
            to = 8 * g + lax.rem(i + d, 8)
            copy = remote(inv_s.at[rows], inv_s.at[rows], sendj.at[0], recvj.at[z], seq=to)
            copy.start()

    def scales_in(z):
        landed(inv_s.at[pl.ds(0, 28)], recvj.at[z])

    query_gain = jnp.broadcast_to(qg_ref[pl.ds(g, 1), :], (128, 128)).T
    key_gain = jnp.broadcast_to(kg_ref[pl.ds(g, 1), :], (128, 128)).T

    def normed(b, i_, g_):
        return xf_s[b].astype(F32) * inv_s[row_at(i_, g_)]

    def prepare(d):
        k = sources[d]
        landed(xf_s.at[pl.ds(0, 4)], recvo.at[d])
        for n in range(8):
            rows = normed(places[d] + n, n, k)
            vt_s[k, :, 128 * n : 128 * n + 128] = rows.astype(BF16)
            kn_s[k, 128 * n : 128 * n + 128, :] = (rows * key_gain).T.astype(BF16)

    own_column(0)
    landed(ss_s.at[pl.ds(0, 3)], sendc.at[0])
    landed(ss_s.at[pl.ds(0, 3)], recvc.at[0])
    total = ss_s[0] + ss_s[1] + ss_s[2] + ss_s[3]
    inv_s[row_at(i, g)] = lax.rsqrt(total / C + EPS)
    mine = inv_s.at[row_at(i, g)]
    for d in range(7, 0, -1):
        copy = remote(mine, mine, sendi.at[0], recvi.at[d // 4], seq=8 * group_at(*OFFSETS[d]) + i)
        copy.start()
    for d in range(1, 4):
        own_column(d)
    scales_out(0)
    for d in range(4, 8):
        own_column(d)
    scales_out(1)
    for d in range(4):
        from_x(d)
    scales_in(0)
    for d in range(4):
        prepare(d)
    for n in range(8):
        q_s[:, 128 * n : 128 * n + 128] = (normed(8 * n + i, i, n) * query_gain).astype(BF16)

    factor = HEAD ** (-0.5) * math.log2(math.e)
    ahead = lax.broadcasted_iota(jnp.int32, (1024, 128), 0) - lax.broadcasted_iota(jnp.int32, (1024, 128), 1)

    def attend(n, segment, carry, masked):
        peak, total, blend = carry
        query = q_s[:, pl.ds(pl.multiple_of(128 * n, 128), 128)]
        score = jnp.dot(kn_s[segment], query, preferred_element_type=F32) * factor
        if masked:
            score = jnp.where(ahead <= 128 * i + 1024 * (n - segment), score, -1e30)
        new_peak = jnp.maximum(peak, jnp.max(score, axis=0, keepdims=True))
        weight = jnp.exp2(score - new_peak)
        shrink = jnp.exp2(peak - new_peak)
        total = total * shrink + jnp.sum(weight, axis=0, keepdims=True)
        blend = blend * shrink + jnp.dot(vt_s[segment], weight.astype(BF16), preferred_element_type=F32)
        return new_peak, total, blend

    def sweep(queries, segments, carries, chains=(3, 2, 1, 0)):
        for j in range(4):
            for m in chains:
                if m < j:
                    continue
                carries[m] = attend(2 * m + queries, 2 * j + segments, carries[m], m == j)
        return carries

    for far in (1, 0):
        carries = [
            (jnp.full((1, 128), -1e30, F32), jnp.zeros((1, 128), F32), jnp.zeros((128, 128), F32))
            for _ in range(4)
        ]
        carries = sweep(lax.rem(half + far, 2), half, carries)
        for m in range(4):
            peak_s[4 * far + m], total_s[4 * far + m], blend_s[4 * far + m] = carries[m]
        from_x(4 + 2 * (1 - far))
        from_x(5 + 2 * (1 - far))
    scales_in(1)
    for d in range(4, 8):
        prepare(d)

    columns = pl.ds(pl.multiple_of(128 * g, 128), 128)

    def given(m, far):
        n = 2 * m + lax.rem(half + far, 2)
        place = 4 * far + m
        return remote(o_s.at[place], out_ref.at[:, columns], sendr.at[0], recvr.at[0], seq=8 * n + i)

    for far, chains in ((1, (1, 0)), (1, (3, 2)), (0, (1, 0)), (0, (3, 2))):
        carries = {m: (peak_s[4 * far + m], total_s[4 * far + m], blend_s[4 * far + m]) for m in chains}
        carries = sweep(lax.rem(half + far, 2), 1 - half, carries, chains)
        for m in chains:
            o_s[4 * far + m] = (carries[m][2] / carries[m][1]).T.astype(BF16)
        for m in chains:
            if far:
                given(m, far).start()
            else:
                pl.when(y != m)(given(m, far).start)
    out_ref[:, columns] = o_s[y]
    landed(o_s.at[pl.ds(0, 7)], recvr.at[0])
    landed(o_s.at[pl.ds(0, 7)], sendr.at[0])
    landed(xf_s.at[pl.ds(0, 7)], senda.at[0])
    landed(xf_s.at[pl.ds(0, 56)], sendx.at[0])
    landed(inv_s.at[pl.ds(0, 7)], sendi.at[0])
    landed(inv_s.at[pl.ds(0, 56)], sendj.at[0])


def finish_kernel(hy_in, out_in, hy_ref, out_ref, semaphores):
    copies = [
        pltpu.make_async_copy(hy_in, hy_ref, semaphores.at[0]),
        pltpu.make_async_copy(out_in, out_ref, semaphores.at[1]),
    ]
    for copy in copies:
        copy.start()
    for copy in copies:
        copy.wait()


def vmem(*shape, dtype=F32):
    return pltpu.VMEM(shape, dtype)


def in_vmem(count):
    return [pl.BlockSpec(memory_space=pltpu.VMEM)] * count


def dmas(count):
    return pltpu.SemaphoreType.DMA((count,))


def on_device(
    token_ids, embedding, short_filter, medium_filter, long_residue, long_rate, query_gain, key_gain
):
    shape = jax.ShapeDtypeStruct
    counts = (2, 2, 1, 1, 1, 1, 1, 1, 1, 1, 1, 2, 1, 2, 1, 1, 8, 8, 8, 1, 1)
    results = pl.pallas_call(
        whole_kernel,
        out_shape=[shape((TOK, 1024), BF16), shape((TOK, 1024), BF16)],
        in_specs=[pl.BlockSpec(memory_space=pl.ANY)] * 8,
        out_specs=in_vmem(2),
        scratch_shapes=[
            vmem(1, 128, dtype=jnp.int32), vmem(512, 1024, dtype=BF16), vmem(7, 1024), vmem(128, 1024),
            vmem(16, 1024), vmem(16, 1024), vmem(8, 128), vmem(8, 128), dmas(8),
            vmem(1, 128, dtype=jnp.int32), vmem(1, 128, dtype=jnp.int32),
            vmem(2176, 128), vmem(2048, 128), vmem(64, 128), vmem(1024, 128), vmem(128, 128), vmem(128, 128),
            vmem(1024, 128), vmem(1024, 128), vmem(128, 128),
            vmem(128, 128), vmem(128, 128), vmem(128, 128), vmem(128, 128), vmem(16, 128),
            vmem(1024, 128), vmem(8, 128, 128, dtype=BF16), vmem(4, 1, 128), vmem(64, 1, 128),
            vmem(64, 128, 128, dtype=BF16), vmem(8, 1024, 128, dtype=BF16), vmem(8, 128, 1024, dtype=BF16),
            vmem(128, 1024, dtype=BF16), vmem(8, 128, 128, dtype=BF16),
            vmem(8, 1, 128), vmem(8, 1, 128), vmem(8, 128, 128),
        ]
        + [dmas(count) for count in counts],
        compiler_params=pltpu.CompilerParams(vmem_limit_bytes=LIMIT, collective_id=0, has_side_effects=True),
        name="whole",
    )(
        token_ids.reshape(1, TOK), embedding, short_filter, medium_filter, long_residue, long_rate,
        query_gain.reshape(8, 128), key_gain.reshape(8, 128),
    )
    return pl.pallas_call(
        finish_kernel,
        out_shape=[shape((TOK, 1024), BF16), shape((TOK, 1024), BF16)],
        in_specs=[pl.BlockSpec(memory_space=pl.ANY)] * 2,
        out_specs=in_vmem(2),
        scratch_shapes=[dmas(2)],
        name="finish",
    )(*results)


def solution(mesh):
    in_specs = (
        P("seq"),
        P(None, "ch"),
        P(None, "ch"),
        P(None, "ch"),
        P(None, "ch"),
        P(None, "ch"),
        P("ch"),
        P("ch"),
    )
    out_specs = (P("seq", "ch"), P("seq", "ch"))
    return jax.shard_map(
        on_device, mesh=mesh, in_specs=in_specs, out_specs=out_specs, check_vma=False
    )
```
